256 devices in a mesh: dp: 32 (over z, y_hi, core), tensor: 8 (over x, y_lo).
Axes of the slice: x: 4, y: 4 (y_hi: 2, y_lo: 2; y = y_hi * 2 + y_lo), z: 8, core: 2. Of those that a mesh axis runs over, the one named last changes fastest.
Arguments:
- tokens: bfloat16 [32768, 2048], P(('dp', 'tensor')), may hold values from -24 to 24
- gain: float32 [2048], replicated, may hold values from 0.1 to 1.9
- w_in: bfloat16 [2048, 3, 2048], P(None, None, 'tensor'), may hold values from -0.125 to 0.125
- w_short: float32 [3, 3, 2048], P(None, None, 'tensor'), may hold values from -3.5 to 3.5
- filters: float32 [128, 128], P('tensor'), may hold values from -0.5 to 0.5
- skip: float32 [2048], P('tensor'), may hold values from 0.5 to 1.5
- w_out: bfloat16 [2048, 2048], P('tensor'), may hold values from -0.125 to 0.125
- cotangent: bfloat16 [32768, 2048], P(('dp', 'tensor')), may hold values from -6 to 6
Outputs:
- mixed: bfloat16 [32768, 2048], P(('dp', 'tensor'))
- token_input_gradient: bfloat16 [32768, 2048], P(('dp', 'tensor'))
- grad_w_in: float32 [2048, 3, 2048], P('dp', None, 'tensor')
- grad_w_out: float32 [2048, 2048], P('tensor', 'dp')
The draws below stay inside these ranges and needn't reach their ends.
All inputs are finite; a program needn't handle non-finite values.
Results may differ from the reference program's by a relative error of at most 0.022.
Values may be sent and summed in bfloat16 or wider, within the bound.
A program may use at most 128 MiB of HBM per device.

```python
import jax
import jax.numpy as jnp
from jax import lax

D = 2048
C = 2048
TAPS = 128
SEQ = 1024
GROUPS = 128
TOKENS = 32768
N_DP = 32
N_TENSOR = 8


def with_spikes(result, own_key, source, target, shards_of, factor):
    owner, partner = [(jnp.arange(result.shape[position]) // (result.shape[position] // shards_of)).reshape([-1 if axis == position else 1 for axis in range(result.ndim)]) for position in (source, target)]
    chosen = jax.random.permutation(own_key, shards_of)[partner]
    strong = (owner == chosen) | (owner == (partner + shards_of // 2) % shards_of)
    return jnp.where(strong, factor * result, result)


def block_levels(stream_key, extent, cuts, low, top_value):
    loudness, own = 1.0, jax.random.fold_in(stream_key, 6)
    for axis_at, shards_of in cuts:
        heights = jnp.exp(jax.random.uniform(jax.random.fold_in(own, axis_at), (shards_of,), jnp.float32, low / len(cuts), top_value / len(cuts)))
        loudness = loudness * jnp.repeat(heights, extent[axis_at] // shards_of).reshape([-1 if axis == axis_at else 1 for axis in range(len(extent))])
    return loudness


def normal_values(rng, shape, scale, most, split=(), held_as=jnp.bfloat16):
    values = jax.random.normal(rng, shape, jnp.float32) * scale
    if len(split) > 0:
        values = block_levels(rng, shape, split, -0.22, 0.18) * values
    return jnp.clip(values, min=-most, max=most).astype(held_as)


def heavy_noise(rng, dims, deviation, most, split, heavy, held_as=jnp.bfloat16):
    result = deviation * jax.random.normal(rng, dims, jnp.float32)
    if split:
        result = result * block_levels(rng, dims, split, -0.22, 0.18)
    return jnp.clip(with_spikes(result, jax.random.fold_in(rng, 3), *heavy), -most, most).astype(held_as)


def setup_inputs(seed: int = 0) -> dict:
    streams_of = jax.random.split(jax.random.key(seed), 9)
    tokens = heavy_noise(streams_of[0], (TOKENS, D), 1.0, 24.0, ((0, 256),), (0, 1, 256, 6.0))
    gain = jnp.clip(1.0 + 0.18 * jax.random.normal(streams_of[1], (D,), jnp.float32), 0.1, 1.9)
    w_in = normal_values(streams_of[2], (D, 3, C), D ** -0.5, 0.125, ((2, 8),))
    w_short = normal_values(streams_of[3], (3, 3, C), 3 ** -0.5, 3.5, ((2, 8),), jnp.float32)
    filters = normal_values(streams_of[4], (GROUPS, TAPS), TAPS ** -0.5, 0.5, ((0, 8),), jnp.float32)
    skip = jnp.clip(0.5 + 1.0 * jax.random.uniform(streams_of[5], (C,), jnp.float32) ** block_levels(streams_of[5], (C,), ((0, 8),), -0.2, 0.2), 0.5, 1.5)
    w_out = normal_values(streams_of[6], (C, D), C ** -0.5, 0.125, ((0, 8),))
    cotangent = normal_values(streams_of[7], (TOKENS, D), 1.0, 6.0, ((0, 256),))
    return dict(tokens=tokens, gain=gain, w_in=w_in, w_short=w_short, filters=filters, skip=skip, w_out=w_out, cotangent=cotangent)


def toeplitz_pair(filters):
    taps = filters.shape[1]
    lag = lax.broadcasted_iota(jnp.int32, (taps, taps), 0) - lax.broadcasted_iota(jnp.int32, (taps, taps), 1)
    extended = jnp.concatenate([filters, jnp.zeros((filters.shape[0], 1), filters.dtype)], axis=1)
    near = extended[:, jnp.where(lag >= 0, lag, taps)]
    far = extended[:, jnp.where(lag < 0, lag + taps, taps)]
    return (near, far)

def causal_conv(signal_rows, near, far):
    length, channels = signal_rows.shape
    groups, taps = (near.shape[0], near.shape[1])
    blocks = signal_rows.reshape(length // taps, taps, groups, channels // groups)
    before = jnp.concatenate([jnp.zeros((1,) + blocks.shape[1:], blocks.dtype), blocks[:-1]], axis=0)
    out = jnp.einsum('gts,bsgc->btgc', near, blocks, precision=lax.Precision.HIGHEST)
    out = out + jnp.einsum('gts,bsgc->btgc', far, before, precision=lax.Precision.HIGHEST)
    return out.reshape(length, channels)

def causal_filter_backward(signal_rows, near, far):
    length, channels = signal_rows.shape
    groups, taps = (near.shape[0], near.shape[1])
    blocks = signal_rows.reshape(length // taps, taps, groups, channels // groups)
    after = jnp.concatenate([blocks[1:], jnp.zeros((1,) + blocks.shape[1:], blocks.dtype)], axis=0)
    out = jnp.einsum('gts,btgc->bsgc', near, blocks, precision=lax.Precision.HIGHEST)
    out = out + jnp.einsum('gts,btgc->bsgc', far, after, precision=lax.Precision.HIGHEST)
    return out.reshape(length, channels)

def delayed(signal_rows, steps):
    return jnp.concatenate([jnp.zeros((steps,) + signal_rows.shape[1:], signal_rows.dtype), signal_rows[:-steps]], axis=0)

def advanced(signal_rows, steps):
    return jnp.concatenate([signal_rows[steps:], jnp.zeros((steps,) + signal_rows.shape[1:], signal_rows.dtype)], axis=0)

def one_sequence(rows, grads, gain, w_in, w_short, near, far, skip, w_out):
    blocks_count = N_TENSOR
    input_float = rows.astype(jnp.float32)
    inverse_deviation = lax.rsqrt(lax.optimization_barrier(jnp.mean(input_float * input_float, axis=-1, keepdims=True)) + 1e-05)
    centered_input = input_float * inverse_deviation
    normed_tokens = (centered_input * gain).astype(jnp.bfloat16)
    z_proj = jnp.einsum('sd,dkc->skc', normed_tokens.astype(jnp.float32), w_in.astype(jnp.float32))
    feature = w_short[0] * z_proj + w_short[1] * delayed(z_proj, 1) + w_short[2] * delayed(z_proj, 2)
    query, key, value = (feature[:, 0], feature[:, 1], feature[:, 2])
    inner = key * value
    conv = causal_conv(inner, near, far) + skip * inner
    gated = (query * conv).astype(jnp.bfloat16)
    gated_blocks = gated.astype(jnp.float32).reshape(SEQ, blocks_count, C // blocks_count)
    out_blocks = w_out.astype(jnp.float32).reshape(blocks_count, C // blocks_count, D)
    mixed_parts = jnp.einsum('snc,ncd->snd', gated_blocks, out_blocks).astype(jnp.bfloat16)
    mixed = lax.optimization_barrier(jnp.sum(mixed_parts.astype(jnp.float32), axis=1)).astype(jnp.bfloat16)
    grad_gated = jnp.dot(grads, w_out.T, preferred_element_type=jnp.float32).astype(jnp.bfloat16)
    part_out = jnp.dot(gated.T, grads, preferred_element_type=jnp.float32)
    grad_g = grad_gated.astype(jnp.float32)
    grad_query = grad_g * conv
    grad_conv = grad_g * query
    grad_inner = causal_filter_backward(grad_conv, near, far) + skip * grad_conv
    grad_feature = jnp.stack([grad_query, grad_inner * value, grad_inner * key], axis=1)
    grad_z = (w_short[0] * grad_feature + w_short[1] * advanced(grad_feature, 1) + w_short[2] * advanced(grad_feature, 2)).astype(jnp.bfloat16)
    part_in = jnp.einsum('sd,skc->dkc', normed_tokens.astype(jnp.float32), grad_z.astype(jnp.float32))
    z_blocks = grad_z.astype(jnp.float32).reshape(SEQ, 3, blocks_count, C // blocks_count)
    in_blocks = w_in.astype(jnp.float32).reshape(D, 3, blocks_count, C // blocks_count)
    normed_parts = jnp.einsum('skni,dkni->snd', z_blocks, in_blocks).astype(jnp.bfloat16)
    grad_normed = lax.optimization_barrier(jnp.sum(normed_parts.astype(jnp.float32), axis=1))
    filter_vector = grad_normed * gain
    token_input_gradient = (inverse_deviation * (filter_vector - centered_input * lax.optimization_barrier(jnp.mean(filter_vector * centered_input, axis=-1, keepdims=True)))).astype(jnp.bfloat16)
    return (mixed, token_input_gradient, part_in, part_out)

def reference(tokens, gain, w_in, w_short, filters, skip, w_out, cotangent):
    near, far = toeplitz_pair(filters)
    rows_all = tokens.reshape(N_DP, SEQ, D)
    grads_all = cotangent.reshape(N_DP, SEQ, D)

    def step(carry, pair):
        mixed, token_input_gradient, part_in, part_out = one_sequence(pair[0], pair[1], gain, w_in, w_short, near, far, skip, w_out)
        return ((carry[0] + part_in, carry[1] + part_out), (mixed, token_input_gradient))
    start = (jnp.zeros((D, 3, C), jnp.float32), jnp.zeros((C, D), jnp.float32))
    totals, outputs = lax.scan(step, start, (rows_all, grads_all))
    scale = 1.0 / float(TOKENS) ** 0.5
    mixed = outputs[0].reshape(TOKENS, D)
    token_input_gradient = outputs[1].reshape(TOKENS, D)
    return (mixed, token_input_gradient, totals[0] * scale, totals[1] * scale)
```

```python
import math

import jax
import jax.numpy as jnp
from jax import lax
from jax.experimental import pallas as pl
from jax.experimental.pallas import tpu as pltpu
from jax.sharding import PartitionSpec as P

MESH = pl.DeviceIdType.MESH
BF = jnp.bfloat16
F32 = jnp.float32
ROWS = 128
HALF = 64
D = 2048
CH = 256
BLOCKS = 8
SEQ = 1024
NZ = 8
SCALE = 1.0 / math.sqrt(32768.0)
NT_DIMS = (((1,), (1,)), ((), ()))


def kernel(
    tok, gain, ws, filt, skip, w3_any, wo_any, cot_any,
    mixed_out, tig_out, gwi_out, gwo_out,
    bufa, bufb, nt, ct, win, wout, zbuf, qkv, ibuf, cbuf, gbuf, ggb, gcb, gz,
    tfwd, tbwd, eye,
    q1, q2, q3, q4, q5,
    grads, cxb, rbuf, ysend, ykeep, yrecv,
    load_sem, ag_s, ag_r, rs_s, rs_r, cx_s, cx_r, ring_s, ring_r, y_s, y_r,
):
    t = lax.axis_index("tensor")
    d = lax.axis_index("dp")
    x, y = lax.div(t, 2), lax.rem(t, 2)
    z, yh, core = lax.div(d, 4), lax.rem(lax.div(d, 2), 2), lax.rem(d, 2)
    xp = {"tensor": lax.rem(x + 1, 4) * 2 + y}
    xm = {"tensor": lax.rem(x + 3, 4) * 2 + y}
    yp = {"tensor": x * 2 + 1 - y}
    zp = {"dp": lax.rem(z + 1, NZ) * 4 + yh * 2 + core}
    zm = {"dp": lax.rem(z + NZ - 1, NZ) * 4 + yh * 2 + core}
    yhp = {"dp": z * 4 + (1 - yh) * 2 + core}
    cp = {"dp": z * 4 + yh * 2 + 1 - core}

    loads = [pltpu.make_async_copy(cot_any, bufb.at[0:ROWS], load_sem.at[0])]
    for j in range(3):
        loads.append(
            pltpu.make_async_copy(
                w3_any.at[j], win.at[:, j * CH : (j + 1) * CH], load_sem.at[1 + j]
            )
        )
    loads.append(pltpu.make_async_copy(wo_any, wout, load_sem.at[4]))
    for c in loads:
        c.start()

    barrier = pltpu.get_barrier_semaphore()
    for dev in (xp, xm, yp, zp, zm, yhp, cp):
        pl.semaphore_signal(barrier, inc=1, device_id=dev, device_id_type=MESH)

    def remote(src, dst, ss, rs, dev):
        return pltpu.make_async_remote_copy(
            src_ref=src, dst_ref=dst, send_sem=ss, recv_sem=rs, device_id=dev, device_id_type=MESH
        )

    def gather_copies(buf, k):
        def rows(slot, lo=0, n=ROWS):
            return buf.at[slot * ROWS + lo : slot * ROWS + lo + n]

        spec = [
            (rows(0), rows(1), yp),
            (rows(0, 0, HALF), rows(6, 0, HALF), xp),
            (rows(0, HALF, HALF), rows(6, HALF, HALF), xp),
            (rows(0, HALF, HALF), rows(2, HALF, HALF), xm),
            (rows(0, 0, HALF), rows(2, 0, HALF), xm),
            (rows(1), rows(7), xp),
            (rows(1), rows(3), xm),
            (rows(6, 0, HALF), rows(4, 0, HALF), xp),
            (rows(2, HALF, HALF), rows(4, HALF, HALF), xm),
            (rows(4), rows(5), yp),
        ]
        return [
            remote(s, e, ag_s.at[k, i], ag_r.at[k, i], dev) for i, (s, e, dev) in enumerate(spec)
        ]

    def scatter_copies(buf, k):
        def rows(slot, lo=0, n=ROWS):
            return buf.at[slot * ROWS + lo : slot * ROWS + lo + n]

        lo, hi = slice(0, HALF), slice(HALF, ROWS)
        spec = [
            (rows(5), q1.at[k], yp),
            (rows(3), q2.at[k, 0], xp),
            (rows(7), q2.at[k, 1], xm),
            (rows(4, HALF, HALF), q3.at[k, 0], xp),
            (rows(4, 0, HALF), q3.at[k, 1], xm),
            (rows(2, 0, HALF), q4.at[k, 0, lo], xp),
            (rows(2, HALF, HALF), q4.at[k, 0, hi], xp),
            (rows(6, HALF, HALF), q4.at[k, 1, hi], xm),
            (rows(6, 0, HALF), q4.at[k, 1, lo], xm),
            (rows(1), q5.at[k], yp),
        ]
        return [
            remote(s, e, rs_s.at[k, i], rs_r.at[k, i], dev) for i, (s, e, dev) in enumerate(spec)
        ]

    def add_rows(buf, row, n, others):
        def step(i, _):
            at = pl.multiple_of(row + i * 16, 16)
            total = buf[pl.ds(at, 16), :].astype(F32)
            for o, shift in others:
                total = total + o[pl.ds(pl.multiple_of(shift + i * 16, 16), 16), :].astype(F32)
            buf[pl.ds(at, 16), :] = total.astype(BF)
            return 0

        lax.fori_loop(0, n // 16, step, 0)

    def add_far(buf, c, k):
        c[0].wait_recv()
        add_rows(buf, 4 * ROWS, ROWS, [(q1.at[k], 0)])
        c[3].start()
        c[4].start()

    def add_side(buf, c, k):
        c[1].wait_recv()
        c[2].wait_recv()
        add_rows(buf, 1 * ROWS, ROWS, [(q2.at[k, 0], 0), (q2.at[k, 1], 0)])
        c[9].start()

    def add_near(buf, c, k):
        c[3].wait_recv()
        add_rows(buf, 2 * ROWS + HALF, HALF, [(q3.at[k, 0], 0)])
        c[6].start()
        c[4].wait_recv()
        add_rows(buf, 6 * ROWS, HALF, [(q3.at[k, 1], 0)])
        c[8].start()

    def wait_last(c):
        for i in (5, 6, 7, 8, 9):
            c[i].wait_recv()

    def last_sum(buf, k, at):
        total = buf[pl.ds(at, 16), :].astype(F32)
        total = total + q4[k, 0, pl.ds(at, 16), :].astype(F32)
        total = total + q4[k, 1, pl.ds(at, 16), :].astype(F32)
        return total + q5[k, pl.ds(at, 16), :].astype(F32)

    def norm(i, _):
        at = pl.multiple_of(i * 16, 16)
        v = tok[pl.ds(at, 16), :].astype(F32)
        r = lax.rsqrt(jnp.mean(v * v, axis=-1, keepdims=True) + 1e-05)
        bufa[pl.ds(at, 16), :] = ((v * r) * gain[...]).astype(BF)
        return 0

    lax.fori_loop(0, ROWS // 16, norm, 0)

    pl.semaphore_wait(barrier, 7)
    ga = gather_copies(bufa, 0)
    gb = gather_copies(bufb, 1)
    for i in (0, 1, 3, 2, 4):
        ga[i].start()

    eye[...] = (
        lax.broadcasted_iota(jnp.int32, (CH, CH), 0) == lax.broadcasted_iota(jnp.int32, (CH, CH), 1)
    ).astype(BF)
    for j in range(3):
        zbuf[j, 0:8, :] = jnp.zeros((8, CH), F32)
    ibuf[0:ROWS, :] = jnp.zeros((ROWS, CH), BF)
    gcb[SEQ : SEQ + ROWS, :] = jnp.zeros((ROWS, CH), BF)

    def tables(g, _):
        row = jnp.concatenate([filt[pl.ds(g, 1), :], jnp.zeros((1, ROWS), F32)], axis=1)
        band = pltpu.roll(
            jnp.broadcast_to(row, (ROWS, 2 * ROWS)), 0, 1, stride=1, stride_axis=0
        ).astype(BF)
        at = pl.multiple_of(g * ROWS, ROWS)
        tbwd[pl.ds(at, ROWS), :] = band
        unit = eye[0:ROWS, 0:ROWS]
        for h in range(2):
            tfwd[pl.ds(at, ROWS), (1 - h) * ROWS : (2 - h) * ROWS] = lax.dot_general(
                unit, band[:, h * ROWS : (h + 1) * ROWS], NT_DIMS, preferred_element_type=F32
            ).astype(BF)
        return 0

    lax.fori_loop(0, 16, tables, 0)

    def seq_rows(p):
        first = lax.rem(x + p, 4) * (2 * ROWS)
        return (
            pl.multiple_of(first, 2 * ROWS),
            pl.multiple_of(first + y * ROWS, ROWS),
            pl.multiple_of(first + (1 - y) * ROWS, ROWS),
        )

    def pair(p):
        return slice(p * 2 * ROWS, (p + 1) * 2 * ROWS)

    def project(p):
        _, r0, r1 = seq_rows(p)
        for j in range(3):
            out = jnp.dot(
                bufa[pair(p), :], win[:, j * CH : (j + 1) * CH], preferred_element_type=F32
            )
            zbuf[j, pl.ds(pl.multiple_of(r0 + 8, 8), ROWS), :] = out[:ROWS]
            zbuf[j, pl.ds(pl.multiple_of(r1 + 8, 8), ROWS), :] = out[ROWS:]

    def turn(src, dst, p):
        _, r0, r1 = seq_rows(p)

        def step(i, _):
            at = pl.multiple_of(i * 256, 256)
            out = lax.dot_general(
                eye[...], src[pair(p), pl.ds(at, 256)], NT_DIMS, preferred_element_type=F32
            ).astype(BF)
            dst[pl.ds(at, 256), pl.ds(r0, ROWS)] = out[:, :ROWS]
            dst[pl.ds(at, 256), pl.ds(r1, ROWS)] = out[:, ROWS:]
            return 0

        lax.fori_loop(0, D // 256, step, 0)

    def back_gate(p):
        _, r0, r1 = seq_rows(p)
        out = lax.dot_general(
            bufb[pair(p), :], wout[...], NT_DIMS, preferred_element_type=F32
        ).astype(BF)
        ggb[pl.ds(r0, ROWS), :] = out[:ROWS]
        ggb[pl.ds(r1, ROWS), :] = out[ROWS:]

    group = lax.shift_right_logical(lax.broadcasted_iota(jnp.int32, (ROWS, ROWS), 1), 4)

    def filtered(table, signal, base):
        outs = []
        for h in range(2):
            big = jnp.dot(
                table[h * 1024 : (h + 1) * 1024, :],
                signal[pl.ds(base, 2 * ROWS), h * ROWS : (h + 1) * ROWS],
                preferred_element_type=F32,
            )
            acc = big[0:ROWS]
            for g in range(1, 8):
                acc = jnp.where(group == g, big[g * ROWS : (g + 1) * ROWS], acc)
            outs.append(acc)
        return jnp.concatenate(outs, axis=1)

    def forward(b, _):
        base = pl.multiple_of(b * ROWS, ROWS)
        f = []
        for j in range(3):
            v = zbuf[j, pl.ds(base, ROWS + 8), :]
            f.append(
                ws[0, j : j + 1, :] * v[8 : 8 + ROWS]
                + ws[1, j : j + 1, :] * v[7 : 7 + ROWS]
                + ws[2, j : j + 1, :] * v[6 : 6 + ROWS]
            )
            qkv[j, pl.ds(base, ROWS), :] = f[j]
        inner = f[1] * f[2]
        ibuf[pl.ds(pl.multiple_of(base + ROWS, ROWS), ROWS), :] = inner.astype(BF)
        conv = filtered(tfwd, ibuf, base) + skip[...] * inner
        cbuf[pl.ds(base, ROWS), :] = conv
        gbuf[pl.ds(base, ROWS), :] = (qkv[0, pl.ds(base, ROWS), :] * conv).astype(BF)
        return 0

    def backward(i, _):
        base = pl.multiple_of((BLOCKS - 1 - i) * ROWS, ROWS)
        here = pl.ds(base, ROWS)
        gg = ggb[here, :].astype(F32)
        gc = gg * qkv[0, here, :]
        gcb[here, :] = gc.astype(BF)
        zbuf[0, here, :] = gg * cbuf[here, :]
        gi = filtered(tbwd, gcb, base) + skip[...] * gc
        zbuf[1, here, :] = gi * qkv[2, here, :]
        zbuf[2, here, :] = gi * qkv[1, here, :]
        for j in range(3):
            v = zbuf[j, pl.ds(base, ROWS + 8), :]
            gz[here, j * CH : (j + 1) * CH] = (
                ws[0, j : j + 1, :] * v[0:ROWS]
                + ws[1, j : j + 1, :] * v[1 : 1 + ROWS]
                + ws[2, j : j + 1, :] * v[2 : 2 + ROWS]
            ).astype(BF)
        return 0

    def mix(p):
        first, _, _ = seq_rows(p)
        at0 = pl.multiple_of(p * 2 * ROWS + y * ROWS, ROWS)
        at1 = pl.multiple_of(p * 2 * ROWS + (1 - y) * ROWS, ROWS)

        def step(i, _):
            cols = pl.ds(pl.multiple_of(i * 512, 512), 512)
            out = jnp.dot(
                gbuf[pl.ds(first, 2 * ROWS), :], wout[:, cols], preferred_element_type=F32
            ).astype(BF)
            bufa[pl.ds(at0, ROWS), cols] = out[:ROWS]
            bufa[pl.ds(at1, ROWS), cols] = out[ROWS:]
            return 0

        lax.fori_loop(0, D // 512, step, 0)

    def back_norm(p):
        first, _, _ = seq_rows(p)
        at0 = pl.multiple_of(p * 2 * ROWS + y * ROWS, ROWS)
        at1 = pl.multiple_of(p * 2 * ROWS + (1 - y) * ROWS, ROWS)

        def step(i, _):
            cols = pl.ds(pl.multiple_of(i * 512, 512), 512)
            out = lax.dot_general(
                gz[pl.ds(first, 2 * ROWS), :], win[cols, :], NT_DIMS, preferred_element_type=F32
            ).astype(BF)
            bufb[pl.ds(at0, ROWS), cols] = out[:ROWS]
            bufb[pl.ds(at1, ROWS), cols] = out[ROWS:]
            return 0

        lax.fori_loop(0, D // 512, step, 0)

    def weight_grad(j, lhs, rhs, col):
        def step(i, _):
            out = jnp.dot(
                lhs[pl.ds(pl.multiple_of(i * 256, 256), 256), :],
                rhs[:, col : col + CH],
                preferred_element_type=F32,
            ).astype(BF)
            for h in range(2):
                for c in range(2):
                    r = (h * 2 + c) * 64
                    grads[c, j, i * 2 + h] = out[r : r + 64]
            return 0

        lax.fori_loop(0, NZ, step, 0)

    cross = [
        remote(grads.at[1 - core, j], cxb.at[j], cx_s.at[j], cx_r.at[j], cp) for j in range(4)
    ]
    hops = [{1: 4 - j % 2, -1: 3 + j % 2} for j in range(4)]
    ring = []
    for j in range(4):
        ring.append({})
        for s in (1, -1):
            n = hops[j][s]
            off = 0 if s == 1 else hops[j][1]
            ring[j][s] = []
            for i in range(n):
                zd = lax.rem(z + s * (n - i) + NZ, NZ)
                ring[j][s].append(
                    (
                        remote(
                            grads.at[core, j, pl.ds(zd * 2, 2)],
                            rbuf.at[j, off + i],
                            ring_s.at[j, off + i],
                            ring_r.at[j, off + i],
                            zp if s == 1 else zm,
                        ),
                        zd,
                        off + i,
                    )
                )

    def cross_add(j):
        cross[j].wait_recv()

        def step(i, _):
            grads[core, j, i] = (grads[core, j, i].astype(F32) + cxb[j, i].astype(F32)).astype(BF)
            return 0

        lax.fori_loop(0, 16, step, 0)

    def ring_round(j, i):
        for s in (1, -1):
            if i >= hops[j][s]:
                continue
            copy, zd, _ = ring[j][s][i]
            if i > 0:
                before, _, k = ring[j][s][i - 1]
                before.wait_recv()
                for h in range(2):
                    at = zd * 2 + h
                    grads[core, j, at] = (
                        grads[core, j, at].astype(F32) + rbuf[j, k, h].astype(F32)
                    ).astype(BF)
            copy.start()

    across = [remote(ysend.at[j], yrecv.at[j], y_s.at[j], y_r.at[j], yhp) for j in range(4)]

    def ring_end(j):
        ends = []
        for s in (1, -1):
            copy, _, k = ring[j][s][hops[j][s] - 1]
            copy.wait_recv()
            ends.append(k)

        def total(h):
            return (
                grads[core, j, z * 2 + h].astype(F32)
                + rbuf[j, ends[0], h].astype(F32)
                + rbuf[j, ends[1], h].astype(F32)
            )

        ysend[j] = total(1 - yh).astype(BF)
        across[j].start()
        ykeep[j] = total(yh)

    ga[1].wait_recv()
    ga[7].start()
    ga[3].wait_recv()
    ga[8].start()
    for c in loads:
        c.wait()
    ga[0].wait_recv()
    ga[5].start()
    ga[6].start()
    for i in (1, 3, 2, 4):
        gb[i].start()
    project(0)
    ga[2].wait_recv()
    ga[4].wait_recv()
    ga[7].wait_recv()
    ga[8].wait_recv()
    ga[9].start()
    gb[0].start()
    turn(bufa, nt, 0)
    ga[5].wait_recv()
    ga[6].wait_recv()
    project(1)
    project(3)
    gb[1].wait_recv()
    gb[7].start()
    gb[3].wait_recv()
    gb[8].start()
    ga[9].wait_recv()
    project(2)
    lax.fori_loop(0, 4, forward, 0)
    gb[0].wait_recv()
    gb[5].start()
    gb[6].start()
    lax.fori_loop(4, 8, forward, 0)
    gb[2].wait_recv()
    gb[4].wait_recv()
    gb[7].wait_recv()
    gb[8].wait_recv()
    gb[9].start()
    turn(bufa, nt, 1)
    turn(bufa, nt, 2)
    turn(bufa, nt, 3)
    for c in ga:
        c.wait_send()
    sa = scatter_copies(bufa, 0)
    mix(2)
    sa[0].start()
    mix(1)
    sa[1].start()
    mix(3)
    sa[2].start()
    sa[5].start()
    sa[7].start()
    mix(0)
    back_gate(0)
    turn(bufb, ct, 0)
    gb[5].wait_recv()
    gb[6].wait_recv()
    back_gate(1)
    back_gate(3)
    gb[9].wait_recv()
    back_gate(2)
    for j in range(3):
        zbuf[j, SEQ : SEQ + 8, :] = jnp.zeros((8, CH), F32)
    lax.fori_loop(0, 8, backward, 0)
    add_far(bufa, sa, 0)
    add_side(bufa, sa, 0)
    turn(bufb, ct, 1)
    turn(bufb, ct, 2)
    turn(bufb, ct, 3)
    for c in gb:
        c.wait_send()
    sb = scatter_copies(bufb, 1)
    back_norm(2)
    sb[0].start()
    back_norm(1)
    sb[1].start()
    back_norm(3)
    sb[2].start()
    sb[5].start()
    sb[7].start()
    back_norm(0)
    weight_grad(3, ct, gbuf, 0)
    cross[3].start()
    add_near(bufa, sa, 0)
    for j in range(3):
        weight_grad(j, nt, gz, j * CH)
        cross[j].start()
    cross_add(3)
    ring_round(3, 0)
    for j in range(3):
        cross_add(j)
        ring_round(j, 0)
    add_far(bufb, sb, 1)
    add_side(bufb, sb, 1)
    for j in (3, 0, 1, 2):
        ring_round(j, 1)
    wait_last(sa)

    def finish_mixed(i, _):
        at = pl.multiple_of(i * 16, 16)
        mixed_out[pl.ds(at, 16), :] = last_sum(bufa, 0, at).astype(BF)
        return 0

    lax.fori_loop(0, ROWS // 16, finish_mixed, 0)
    for j in (3, 0, 1, 2):
        ring_round(j, 2)
    add_near(bufb, sb, 1)
    for j in (3, 0, 1, 2):
        ring_round(j, 3)
    for j in (3, 0, 1, 2):
        ring_end(j)
    wait_last(sb)

    def finish_tokens(i, _):
        at = pl.multiple_of(i * 16, 16)
        v = tok[pl.ds(at, 16), :].astype(F32)
        r = lax.rsqrt(jnp.mean(v * v, axis=-1, keepdims=True) + 1e-05)
        xhat = v * r
        h = last_sum(bufb, 1, at) * gain[...]
        tig_out[pl.ds(at, 16), :] = (
            r * (h - xhat * jnp.mean(h * xhat, axis=-1, keepdims=True))
        ).astype(BF)
        return 0

    lax.fori_loop(0, ROWS // 16, finish_tokens, 0)
    for j in (3, 0, 1, 2):
        across[j].wait_recv()
        out = (ykeep[j] + yrecv[j].astype(F32)) * SCALE
        if j == 3:
            gwo_out[...] = out
        else:
            gwi_out[j] = out
    for c in sa + sb + cross + across:
        c.wait_send()
    for j in range(4):
        for s in (1, -1):
            for c, _, _ in ring[j][s]:
                c.wait_send()


def body(tokens, gain, w_in, w_short, filters, skip, w_out, cotangent):
    vmem = pl.BlockSpec(memory_space=pltpu.VMEM)
    away = pl.BlockSpec(memory_space=pl.ANY)
    dma = pltpu.SemaphoreType.DMA
    mixed, token_grad, gwi, gwo = pl.pallas_call(
        kernel,
        out_shape=(
            jax.ShapeDtypeStruct((ROWS, D), BF),
            jax.ShapeDtypeStruct((ROWS, D), BF),
            jax.ShapeDtypeStruct((3, 64, CH), F32),
            jax.ShapeDtypeStruct((64, CH), F32),
        ),
        in_specs=[vmem] * 5 + [away] * 3,
        out_specs=(vmem,) * 4,
        scratch_shapes=[
            pltpu.VMEM((SEQ, D), BF),
            pltpu.VMEM((SEQ, D), BF),
            pltpu.VMEM((D, SEQ), BF),
            pltpu.VMEM((D, SEQ), BF),
            pltpu.VMEM((D, 3 * CH), BF),
            pltpu.VMEM((CH, D), BF),
            pltpu.VMEM((3, SEQ + 8, CH), F32),
            pltpu.VMEM((3, SEQ, CH), F32),
            pltpu.VMEM((SEQ + ROWS, CH), BF),
            pltpu.VMEM((SEQ, CH), F32),
            pltpu.VMEM((SEQ, CH), BF),
            pltpu.VMEM((SEQ, CH), BF),
            pltpu.VMEM((SEQ + ROWS, CH), BF),
            pltpu.VMEM((SEQ, 3 * CH), BF),
            pltpu.VMEM((2048, 256), BF),
            pltpu.VMEM((2048, 256), BF),
            pltpu.VMEM((CH, CH), BF),
            pltpu.VMEM((2, ROWS, D), BF),
            pltpu.VMEM((2, 2, ROWS, D), BF),
            pltpu.VMEM((2, 2, HALF, D), BF),
            pltpu.VMEM((2, 2, ROWS, D), BF),
            pltpu.VMEM((2, ROWS, D), BF),
            pltpu.VMEM((2, 4, 16, 64, CH), BF),
            pltpu.VMEM((4, 16, 64, CH), BF),
            pltpu.VMEM((4, 7, 2, 64, CH), BF),
            pltpu.VMEM((4, 64, CH), BF),
            pltpu.VMEM((4, 64, CH), F32),
            pltpu.VMEM((4, 64, CH), BF),
            dma((5,)),
            dma((2, 10)),
            dma((2, 10)),
            dma((2, 10)),
            dma((2, 10)),
            dma((4,)),
            dma((4,)),
            dma((4, 7)),
            dma((4, 7)),
            dma((4,)),
            dma((4,)),
        ],
        compiler_params=pltpu.CompilerParams(
            collective_id=0, has_side_effects=True, vmem_limit_bytes=67043328
        ),
        name="hyena_block",
    )(
        tokens,
        gain.reshape(1, D),
        w_short,
        filters,
        skip.reshape(1, CH),
        jnp.transpose(w_in, (1, 0, 2)),
        w_out,
        cotangent,
    )
    return mixed, token_grad, jnp.transpose(gwi, (1, 0, 2)), gwo.T


def solution(mesh):
    return jax.shard_map(
        body,
        mesh=mesh,
        in_specs=(
            P(("dp", "tensor"), None),
            P(None),
            P(None, None, "tensor"),
            P(None, None, "tensor"),
            P("tensor", None),
            P("tensor"),
            P("tensor", None),
            P(("dp", "tensor"), None),
        ),
        out_specs=(
            P(("dp", "tensor"), None),
            P(("dp", "tensor"), None),
            P("dp", None, "tensor"),
            P("tensor", "dp"),
        ),
        check_vma=False,
    )
```

```python
import math

import jax
import jax.numpy as jnp
from jax import lax
from jax.experimental import pallas as pl
from jax.experimental.pallas import tpu as pltpu
from jax.sharding import PartitionSpec as P

MESH = pl.DeviceIdType.MESH
BF = jnp.bfloat16
F32 = jnp.float32
ROWS = 128
HALF = 64
DH = 1024
D = 2048
CH = 256
BLOCKS = 8
SEQ = 1024
NZ = 8
SCALE = 1.0 / math.sqrt(32768.0)
NT_DIMS = (((1,), (1,)), ((), ()))


def kernel(
    tok, gain, ws, filt, skip, w3_any, wo_any, cot_any,
    mixed_out, tig_out, gwi_out, gwo_out,
    bufa, chalf, mpart, nt, ct, win, wmine, wother, zbuf, qkv, ibuf, cbuf, gbuf, gother,
    ggmine, ggsend, ggother, gcb, gz, tfwd, tbwd, eye,
    q1, q2, q3, q4, q5, n3, n4, nsend, n5,
    grads, gout, cxb, rbuf, ysend, ykeep, yrecv,
    load_sem, n_s, n_r, c_s, c_r, w_s, w_r, ga_s, ga_r, gg_s, gg_r, m_s, m_r, t_s, t_r,
    go_s, go_r, cx_s, cx_r, ring_s, ring_r, y_s, y_r,
):
    t = lax.axis_index("tensor")
    d = lax.axis_index("dp")
    x, y = lax.div(t, 2), lax.rem(t, 2)
    z, yh, core = lax.div(d, 4), lax.rem(lax.div(d, 2), 2), lax.rem(d, 2)
    xp = {"tensor": lax.rem(x + 1, 4) * 2 + y}
    xm = {"tensor": lax.rem(x + 3, 4) * 2 + y}
    yp = {"tensor": x * 2 + 1 - y}
    zp = {"dp": lax.rem(z + 1, NZ) * 4 + yh * 2 + core}
    zm = {"dp": lax.rem(z + NZ - 1, NZ) * 4 + yh * 2 + core}
    outer = {"dp": z * 4 + (1 - yh) * 2 + core, "tensor": x * 2 + 1 - y}
    yhp = {"dp": z * 4 + (1 - yh) * 2 + core}
    cp = {"dp": z * 4 + yh * 2 + 1 - core}

    my_half = pl.ds(pl.multiple_of(y * DH, DH), DH)
    other_half = pl.ds(pl.multiple_of((1 - y) * DH, DH), DH)
    loads = [pltpu.make_async_copy(cot_any.at[:, my_half], chalf.at[0:ROWS], load_sem.at[0])]
    for j in range(3):
        loads.append(
            pltpu.make_async_copy(
                w3_any.at[j], win.at[:, j * CH : (j + 1) * CH], load_sem.at[1 + j]
            )
        )
    loads.append(pltpu.make_async_copy(wo_any.at[:, my_half], wmine, load_sem.at[4]))
    for c in loads:
        c.start()

    barrier = pltpu.get_barrier_semaphore()
    for dev in (xp, xm, yp, zp, zm, yhp, cp, outer):
        pl.semaphore_signal(barrier, inc=1, device_id=dev, device_id_type=MESH)

    def remote(src, dst, ss, rs, dev):
        return pltpu.make_async_remote_copy(
            src_ref=src, dst_ref=dst, send_sem=ss, recv_sem=rs, device_id=dev, device_id_type=MESH
        )

    def gather_copies(buf):
        def rows(slot, lo=0, n=ROWS):
            return buf.at[slot * ROWS + lo : slot * ROWS + lo + n]

        spec = [
            (rows(0), rows(1), yp),
            (rows(0, 0, HALF), rows(6, 0, HALF), xp),
            (rows(0, HALF, HALF), rows(6, HALF, HALF), xp),
            (rows(0, HALF, HALF), rows(2, HALF, HALF), xm),
            (rows(0, 0, HALF), rows(2, 0, HALF), xm),
            (rows(1), rows(7), xp),
            (rows(1), rows(3), xm),
            (rows(6, 0, HALF), rows(4, 0, HALF), xp),
            (rows(2, HALF, HALF), rows(4, HALF, HALF), xm),
            (rows(4), rows(5), yp),
        ]
        return [
            remote(s, e, n_s.at[i], n_r.at[i], dev) for i, (s, e, dev) in enumerate(spec)
        ]

    def half_copies():
        def rows(slot):
            return chalf.at[slot * ROWS : (slot + 1) * ROWS]

        spec = [
            (cot_any.at[:, other_half], rows(1), yp),
            (rows(0), rows(6), xp),
            (rows(1), rows(7), xp),
            (rows(1), rows(3), xm),
            (rows(0), rows(2), xm),
            (rows(6), rows(4), xp),
            (rows(3), rows(5), xm),
        ]
        return [remote(s, e, c_s.at[i], c_r.at[i], dev) for i, (s, e, dev) in enumerate(spec)]

    def mixed_copies():
        def rows(p, b):
            at = (2 * p + b) * ROWS
            return mpart.at[at : at + ROWS]

        spec = [
            (rows(2, 1), n3.at[0], xp),
            (rows(2, 0), n3.at[1], xm),
            (rows(1, 0), n4.at[0, 0], xp),
            (rows(1, 1), n4.at[0, 1], xp),
            (rows(3, 1), n4.at[1, 1], xm),
            (rows(3, 0), n4.at[1, 0], xm),
            (nsend, n5, yp),
        ]
        return [remote(s, e, m_s.at[i], m_r.at[i], dev) for i, (s, e, dev) in enumerate(spec)]

    def scatter_copies(buf):
        def rows(slot, lo=0, n=ROWS):
            return buf.at[slot * ROWS + lo : slot * ROWS + lo + n]

        lo, hi = slice(0, HALF), slice(HALF, ROWS)
        spec = [
            (rows(5), q1, yp),
            (rows(3), q2.at[0], xp),
            (rows(7), q2.at[1], xm),
            (rows(4, HALF, HALF), q3.at[0], xp),
            (rows(4, 0, HALF), q3.at[1], xm),
            (rows(2, 0, HALF), q4.at[0, lo], xp),
            (rows(2, HALF, HALF), q4.at[0, hi], xp),
            (rows(6, HALF, HALF), q4.at[1, hi], xm),
            (rows(6, 0, HALF), q4.at[1, lo], xm),
            (rows(1), q5, yp),
        ]
        return [
            remote(s, e, t_s.at[i], t_r.at[i], dev) for i, (s, e, dev) in enumerate(spec)
        ]

    def add_rows(buf, row, n, others):
        def step(i, _):
            at = pl.multiple_of(row + i * 16, 16)
            total = buf[pl.ds(at, 16), :].astype(F32)
            for o, shift in others:
                total = total + o[pl.ds(pl.multiple_of(shift + i * 16, 16), 16), :].astype(F32)
            buf[pl.ds(at, 16), :] = total.astype(BF)
            return 0

        lax.fori_loop(0, n // 16, step, 0)

    def add_far(buf, c):
        c[0].wait_recv()
        add_rows(buf, 4 * ROWS, ROWS, [(q1, 0)])
        c[3].start()
        c[4].start()

    def add_side(buf, c):
        c[1].wait_recv()
        c[2].wait_recv()
        add_rows(buf, 1 * ROWS, ROWS, [(q2.at[0], 0), (q2.at[1], 0)])
        c[9].start()

    def add_near(buf, c):
        c[3].wait_recv()
        add_rows(buf, 2 * ROWS + HALF, HALF, [(q3.at[0], 0)])
        c[6].start()
        c[4].wait_recv()
        add_rows(buf, 6 * ROWS, HALF, [(q3.at[1], 0)])
        c[8].start()

    def wait_last(c):
        for i in (5, 6, 7, 8, 9):
            c[i].wait_recv()

    def last_sum(buf, at):
        total = buf[pl.ds(at, 16), :].astype(F32)
        total = total + q4[0, pl.ds(at, 16), :].astype(F32)
        total = total + q4[1, pl.ds(at, 16), :].astype(F32)
        return total + q5[pl.ds(at, 16), :].astype(F32)

    def norm(i, _):
        at = pl.multiple_of(i * 16, 16)
        v = tok[pl.ds(at, 16), :].astype(F32)
        r = lax.rsqrt(jnp.mean(v * v, axis=-1, keepdims=True) + 1e-05)
        bufa[pl.ds(at, 16), :] = ((v * r) * gain[...]).astype(BF)
        return 0

    lax.fori_loop(0, ROWS // 16, norm, 0)

    pl.semaphore_wait(barrier, 8)
    ga = gather_copies(bufa)
    gc_ = half_copies()
    wx = remote(wo_any.at[:, other_half], wother, w_s.at[0], w_r.at[0], outer)
    for i in (0, 1, 3, 2, 4):
        ga[i].start()
    gc_[0].start()
    wx.start()

    eye[...] = (
        lax.broadcasted_iota(jnp.int32, (CH, CH), 0) == lax.broadcasted_iota(jnp.int32, (CH, CH), 1)
    ).astype(BF)
    for j in range(3):
        zbuf[j, 0:8, :] = jnp.zeros((8, CH), F32)
    ibuf[0:ROWS, :] = jnp.zeros((ROWS, CH), BF)
    gcb[SEQ : SEQ + ROWS, :] = jnp.zeros((ROWS, CH), BF)

    def tables(g, _):
        row = jnp.concatenate([filt[pl.ds(g, 1), :], jnp.zeros((1, ROWS), F32)], axis=1)
        band = pltpu.roll(
            jnp.broadcast_to(row, (ROWS, 2 * ROWS)), 0, 1, stride=1, stride_axis=0
        ).astype(BF)
        at = pl.multiple_of(g * ROWS, ROWS)
        tbwd[pl.ds(at, ROWS), :] = band
        unit = eye[0:ROWS, 0:ROWS]
        for h in range(2):
            tfwd[pl.ds(at, ROWS), (1 - h) * ROWS : (2 - h) * ROWS] = lax.dot_general(
                unit, band[:, h * ROWS : (h + 1) * ROWS], NT_DIMS, preferred_element_type=F32
            ).astype(BF)
        return 0

    lax.fori_loop(0, 16, tables, 0)

    def seq_rows(p):
        first = lax.rem(x + p, 4) * (2 * ROWS)
        return (
            pl.multiple_of(first, 2 * ROWS),
            pl.multiple_of(first + y * ROWS, ROWS),
            pl.multiple_of(first + (1 - y) * ROWS, ROWS),
        )

    def pair(p):
        return slice(p * 2 * ROWS, (p + 1) * 2 * ROWS)

    def project(p):
        _, r0, r1 = seq_rows(p)
        for j in range(3):
            out = jnp.dot(
                bufa[pair(p), :], win[:, j * CH : (j + 1) * CH], preferred_element_type=F32
            )
            zbuf[j, pl.ds(pl.multiple_of(r0 + 8, 8), ROWS), :] = out[:ROWS]
            zbuf[j, pl.ds(pl.multiple_of(r1 + 8, 8), ROWS), :] = out[ROWS:]

    def turn(src, dst, p):
        _, r0, r1 = seq_rows(p)

        def step(i, _):
            at = pl.multiple_of(i * 256, 256)
            out = lax.dot_general(
                eye[...], src[pair(p), pl.ds(at, 256)], NT_DIMS, preferred_element_type=F32
            ).astype(BF)
            dst[pl.ds(at, 256), pl.ds(r0, ROWS)] = out[:, :ROWS]
            dst[pl.ds(at, 256), pl.ds(r1, ROWS)] = out[:, ROWS:]
            return 0

        lax.fori_loop(0, dst.shape[0] // 256, step, 0)

    def exchange(src, dst, ss, rs):
        out = []
        for p in range(4):
            rows = pl.ds(p * 2 * ROWS, 2 * ROWS)
            out.append(remote(src.at[rows], dst.at[rows], ss.at[p], rs.at[p], yp))
        return out

    gated_x = exchange(gbuf, gother, ga_s, ga_r)
    gate_x = []
    for p in range(4):
        rows = pl.ds(seq_rows(p)[0], 2 * ROWS)
        gate_x.append(
            remote(ggsend.at[rows], ggother.at[rows], gg_s.at[p], gg_r.at[p], yp)
        )

    def back_gate(p):
        _, r0, r1 = seq_rows(p)
        for w, dst, kind in ((wother, ggsend, BF), (wmine, ggmine, F32)):
            out = lax.dot_general(
                chalf[pair(p), :], w[...], NT_DIMS, preferred_element_type=F32
            ).astype(kind)
            dst[pl.ds(r0, ROWS), :] = out[:ROWS]
            dst[pl.ds(r1, ROWS), :] = out[ROWS:]
        gate_x[p].start()

    group = lax.shift_right_logical(lax.broadcasted_iota(jnp.int32, (ROWS, ROWS), 1), 4)

    def filtered(table, signal, base):
        outs = []
        for h in range(2):
            big = jnp.dot(
                table[h * 1024 : (h + 1) * 1024, :],
                signal[pl.ds(base, 2 * ROWS), h * ROWS : (h + 1) * ROWS],
                preferred_element_type=F32,
            )
            acc = big[0:ROWS]
            for g in range(1, 8):
                acc = jnp.where(group == g, big[g * ROWS : (g + 1) * ROWS], acc)
            outs.append(acc)
        return jnp.concatenate(outs, axis=1)

    def forward(b, _):
        base = pl.multiple_of(b * ROWS, ROWS)
        f = []
        for j in range(3):
            v = zbuf[j, pl.ds(base, ROWS + 8), :]
            f.append(
                ws[0, j : j + 1, :] * v[8 : 8 + ROWS]
                + ws[1, j : j + 1, :] * v[7 : 7 + ROWS]
                + ws[2, j : j + 1, :] * v[6 : 6 + ROWS]
            )
            qkv[j, pl.ds(base, ROWS), :] = f[j]
        inner = f[1] * f[2]
        ibuf[pl.ds(pl.multiple_of(base + ROWS, ROWS), ROWS), :] = inner.astype(BF)
        conv = filtered(tfwd, ibuf, base) + skip[...] * inner
        cbuf[pl.ds(base, ROWS), :] = conv
        gbuf[pl.ds(base, ROWS), :] = (qkv[0, pl.ds(base, ROWS), :] * conv).astype(BF)
        return 0

    def backward(i, _):
        base = pl.multiple_of((BLOCKS - 1 - i) * ROWS, ROWS)
        here = pl.ds(base, ROWS)
        gg = (ggmine[here, :] + ggother[here, :].astype(F32)).astype(BF).astype(F32)
        gc = gg * qkv[0, here, :]
        gcb[here, :] = gc.astype(BF)
        zbuf[0, here, :] = gg * cbuf[here, :]
        gi = filtered(tbwd, gcb, base) + skip[...] * gc
        zbuf[1, here, :] = gi * qkv[2, here, :]
        zbuf[2, here, :] = gi * qkv[1, here, :]
        for j in range(3):
            v = zbuf[j, pl.ds(base, ROWS + 8), :]
            gz[here, j * CH : (j + 1) * CH] = (
                ws[0, j : j + 1, :] * v[0:ROWS]
                + ws[1, j : j + 1, :] * v[1 : 1 + ROWS]
                + ws[2, j : j + 1, :] * v[2 : 2 + ROWS]
            ).astype(BF)
        return 0

    def mix(p):
        rows = pl.ds(seq_rows(p)[0], 2 * ROWS)

        def step(i, _):
            cols = pl.ds(pl.multiple_of(i * 512, 512), 512)
            out = jnp.dot(gbuf[rows, :], wmine[:, cols], preferred_element_type=F32)
            out = out + jnp.dot(gother[rows, :], wother[:, cols], preferred_element_type=F32)
            mpart[p * 2 * ROWS : (p + 1) * 2 * ROWS, cols] = out.astype(BF)
            return 0

        lax.fori_loop(0, DH // 512, step, 0)

    def back_norm(p):
        first, _, _ = seq_rows(p)
        at0 = pl.multiple_of(p * 2 * ROWS + y * ROWS, ROWS)
        at1 = pl.multiple_of(p * 2 * ROWS + (1 - y) * ROWS, ROWS)

        def step(i, _):
            cols = pl.ds(pl.multiple_of(i * 512, 512), 512)
            out = lax.dot_general(
                gz[pl.ds(first, 2 * ROWS), :], win[cols, :], NT_DIMS, preferred_element_type=F32
            ).astype(BF)
            bufa[pl.ds(at0, ROWS), cols] = out[:ROWS]
            bufa[pl.ds(at1, ROWS), cols] = out[ROWS:]
            return 0

        lax.fori_loop(0, D // 512, step, 0)

    def weight_grad(j, lhs, rhs, col):
        def step(i, _):
            out = jnp.dot(
                lhs[pl.ds(pl.multiple_of(i * 256, 256), 256), :],
                rhs[:, col : col + CH],
                preferred_element_type=F32,
            ).astype(BF)
            for h in range(2):
                for c in range(2):
                    r = (h * 2 + c) * 64
                    grads[c, j, i * 2 + h] = out[r : r + 64]
            return 0

        lax.fori_loop(0, NZ, step, 0)

    def weight_grad_out():
        def step(i, _):
            lhs = ct[pl.ds(pl.multiple_of(i * 256, 256), 256), :]
            mine = jnp.dot(lhs, gbuf[...], preferred_element_type=F32).astype(BF)
            other = jnp.dot(lhs, gother[...], preferred_element_type=F32).astype(BF)
            for h in range(2):
                for c in range(2):
                    r = (h * 2 + c) * 64
                    grads[c, 3, y * 8 + i * 2 + h] = mine[r : r + 64]
                    gout[c, i * 2 + h] = other[r : r + 64]
            return 0

        lax.fori_loop(0, 4, step, 0)

    out_x = [
        remote(gout.at[c], grads.at[c, 3, pl.ds(y * 8, 8)], go_s.at[c], go_r.at[c], outer)
        for c in range(2)
    ]

    cross = [
        remote(grads.at[1 - core, j], cxb.at[j], cx_s.at[j], cx_r.at[j], cp) for j in range(4)
    ]
    hops = [{1: 4 - j % 2, -1: 3 + j % 2} for j in range(4)]
    ring = []
    for j in range(4):
        ring.append({})
        for s in (1, -1):
            n = hops[j][s]
            off = 0 if s == 1 else hops[j][1]
            ring[j][s] = []
            for i in range(n):
                zd = lax.rem(z + s * (n - i) + NZ, NZ)
                ring[j][s].append(
                    (
                        remote(
                            grads.at[core, j, pl.ds(zd * 2, 2)],
                            rbuf.at[j, off + i],
                            ring_s.at[j, off + i],
                            ring_r.at[j, off + i],
                            zp if s == 1 else zm,
                        ),
                        zd,
                        off + i,
                    )
                )

    def cross_add(j):
        cross[j].wait_recv()

        def step(i, _):
            grads[core, j, i] = (grads[core, j, i].astype(F32) + cxb[j, i].astype(F32)).astype(BF)
            return 0

        lax.fori_loop(0, 16, step, 0)

    def ring_round(j, i):
        for s in (1, -1):
            if i >= hops[j][s]:
                continue
            copy, zd, _ = ring[j][s][i]
            if i > 0:
                before, _, k = ring[j][s][i - 1]
                before.wait_recv()
                for h in range(2):
                    at = zd * 2 + h
                    grads[core, j, at] = (
                        grads[core, j, at].astype(F32) + rbuf[j, k, h].astype(F32)
                    ).astype(BF)
            copy.start()

    across = [remote(ysend.at[j], yrecv.at[j], y_s.at[j], y_r.at[j], yhp) for j in range(4)]

    def ring_end(j):
        ends = []
        for s in (1, -1):
            copy, _, k = ring[j][s][hops[j][s] - 1]
            copy.wait_recv()
            ends.append(k)

        def total(h):
            return (
                grads[core, j, z * 2 + h].astype(F32)
                + rbuf[j, ends[0], h].astype(F32)
                + rbuf[j, ends[1], h].astype(F32)
            )

        ysend[j] = total(1 - yh).astype(BF)
        across[j].start()
        ykeep[j] = total(yh)

    def add_cols(row, other):
        def step(i, _):
            at = pl.multiple_of(row + i * 32, 32)
            mpart[pl.ds(at, 32), :] = (
                mpart[pl.ds(at, 32), :].astype(F32)
                + other[pl.ds(pl.multiple_of(i * 32, 32), 32), :].astype(F32)
            ).astype(BF)
            return 0

        lax.fori_loop(0, ROWS // 32, step, 0)

    def mixed_sum(b, i):
        at = pl.ds(pl.multiple_of(b * ROWS + i * 32, 32), 32)
        here = pl.ds(pl.multiple_of(i * 32, 32), 32)
        return (
            mpart[at, :].astype(F32)
            + n4[0, b, here, :].astype(F32)
            + n4[1, b, here, :].astype(F32)
        ).astype(BF), here

    def mixed_other(i, _):
        out, here = mixed_sum(1 - y, i)
        nsend[here, :] = out
        return 0

    def mixed_mine(i, _):
        out, here = mixed_sum(y, i)
        mixed_out[here, my_half] = out
        return 0

    ga[1].wait_recv()
    ga[7].start()
    ga[3].wait_recv()
    ga[8].start()
    for c in loads:
        c.wait()
    ga[0].wait_recv()
    ga[5].start()
    ga[6].start()
    project(0)
    gc_[0].wait_recv()
    for i in (1, 3, 2, 4):
        gc_[i].start()
    ga[2].wait_recv()
    ga[4].wait_recv()
    ga[7].wait_recv()
    ga[8].wait_recv()
    ga[9].start()
    wx.wait_recv()
    turn(bufa, nt, 0)
    back_gate(0)
    turn(chalf, ct, 0)
    ga[5].wait_recv()
    ga[6].wait_recv()
    project(1)
    project(3)
    ga[9].wait_recv()
    project(2)
    for p in range(4):
        lax.fori_loop(2 * p, 2 * p + 2, forward, 0)
        gated_x[p].start()
    gc_[1].wait_recv()
    gc_[5].start()
    gc_[3].wait_recv()
    gc_[6].start()
    for p in range(1, 4):
        turn(bufa, nt, p)
    gc_[4].wait_recv()
    back_gate(1)
    gc_[2].wait_recv()
    back_gate(3)
    turn(chalf, ct, 1)
    turn(chalf, ct, 3)
    for j in range(3):
        zbuf[j, SEQ : SEQ + 8, :] = jnp.zeros((8, CH), F32)
    gc_[5].wait_recv()
    gc_[6].wait_recv()
    back_gate(2)
    for p in range(4):
        gated_x[p].wait_recv()
    ma = mixed_copies()
    mix(2)
    ma[0].start()
    ma[1].start()
    mix(1)
    ma[2].start()
    mix(3)
    ma[4].start()
    mix(0)
    turn(chalf, ct, 2)
    weight_grad_out()
    for c in out_x:
        c.start()
    for c in ga:
        c.wait_send()
    for p in range(4):
        gate_x[p].wait_recv()
    lax.fori_loop(0, 4, backward, 0)
    ma[0].wait_recv()
    add_cols(3 * ROWS, n3.at[0])
    ma[3].start()
    ma[1].wait_recv()
    add_cols(6 * ROWS, n3.at[1])
    ma[5].start()
    lax.fori_loop(4, 8, backward, 0)
    sb = scatter_copies(bufa)
    back_norm(2)
    sb[0].start()
    back_norm(1)
    sb[1].start()
    back_norm(3)
    sb[2].start()
    back_norm(0)
    for i in (2, 3, 4, 5):
        ma[i].wait_recv()
    lax.fori_loop(0, 4, mixed_other, 0)
    ma[6].start()
    lax.fori_loop(0, 4, mixed_mine, 0)
    for c in out_x:
        c.wait_recv()
    cross[3].start()
    weight_grad(0, nt, gz, 0)
    cross[0].start()
    cross_add(3)
    ring_round(3, 0)
    weight_grad(1, nt, gz, CH)
    cross[1].start()
    cross_add(0)
    ring_round(0, 0)
    add_far(bufa, sb)
    sb[5].start()
    sb[7].start()
    weight_grad(2, nt, gz, 2 * CH)
    cross[2].start()
    ring_round(3, 1)
    cross_add(1)
    ring_round(1, 0)
    add_side(bufa, sb)
    cross_add(2)
    ring_round(2, 0)
    ring_round(0, 1)
    ring_round(3, 2)
    ring_round(1, 1)
    add_near(bufa, sb)
    ma[6].wait_recv()
    mixed_out[:, other_half] = n5[...]
    for j, i in ((2, 1), (0, 2), (3, 3), (1, 2), (2, 2), (0, 3), (1, 3)):
        ring_round(j, i)
    ring_end(3)
    ring_round(2, 3)
    for j in (0, 1, 2):
        ring_end(j)
    wait_last(sb)

    def finish_tokens(i, _):
        at = pl.multiple_of(i * 16, 16)
        v = tok[pl.ds(at, 16), :].astype(F32)
        r = lax.rsqrt(jnp.mean(v * v, axis=-1, keepdims=True) + 1e-05)
        xhat = v * r
        h = last_sum(bufa, at) * gain[...]
        tig_out[pl.ds(at, 16), :] = (
            r * (h - xhat * jnp.mean(h * xhat, axis=-1, keepdims=True))
        ).astype(BF)
        return 0

    lax.fori_loop(0, ROWS // 16, finish_tokens, 0)
    for j in (3, 0, 1, 2):
        across[j].wait_recv()
        out = (ykeep[j] + yrecv[j].astype(F32)) * SCALE
        if j == 3:
            gwo_out[...] = out
        else:
            gwi_out[j] = out
    for c in gc_ + [wx] + gated_x + gate_x + ma + sb + out_x + cross + across:
        c.wait_send()
    for j in range(4):
        for s in (1, -1):
            for c, _, _ in ring[j][s]:
                c.wait_send()


def place(a, b, c, d, oa, ob, oc, od):
    for src, dst in ((a, oa), (b, ob), (c, oc), (d, od)):
        dst[...] = src[...]


def body(tokens, gain, w_in, w_short, filters, skip, w_out, cotangent):
    vmem = pl.BlockSpec(memory_space=pltpu.VMEM)
    away = pl.BlockSpec(memory_space=pl.ANY)
    dma = pltpu.SemaphoreType.DMA
    mixed, token_grad, gwi, gwo = pl.pallas_call(
        kernel,
        out_shape=(
            jax.ShapeDtypeStruct((ROWS, D), BF),
            jax.ShapeDtypeStruct((ROWS, D), BF),
            jax.ShapeDtypeStruct((3, 64, CH), F32),
            jax.ShapeDtypeStruct((64, CH), F32),
        ),
        in_specs=[vmem] * 5 + [away] * 3,
        out_specs=(vmem,) * 4,
        scratch_shapes=[
            pltpu.VMEM((SEQ, D), BF),
            pltpu.VMEM((SEQ, DH), BF),
            pltpu.VMEM((SEQ, DH), BF),
            pltpu.VMEM((D, SEQ), BF),
            pltpu.VMEM((DH, SEQ), BF),
            pltpu.VMEM((D, 3 * CH), BF),
            pltpu.VMEM((CH, DH), BF),
            pltpu.VMEM((CH, DH), BF),
            pltpu.VMEM((3, SEQ + 8, CH), F32),
            pltpu.VMEM((3, SEQ, CH), F32),
            pltpu.VMEM((SEQ + ROWS, CH), BF),
            pltpu.VMEM((SEQ, CH), F32),
            pltpu.VMEM((SEQ, CH), BF),
            pltpu.VMEM((SEQ, CH), BF),
            pltpu.VMEM((SEQ, CH), F32),
            pltpu.VMEM((SEQ, CH), BF),
            pltpu.VMEM((SEQ, CH), BF),
            pltpu.VMEM((SEQ + ROWS, CH), BF),
            pltpu.VMEM((SEQ, 3 * CH), BF),
            pltpu.VMEM((2048, 256), BF),
            pltpu.VMEM((2048, 256), BF),
            pltpu.VMEM((CH, CH), BF),
            pltpu.VMEM((ROWS, D), BF),
            pltpu.VMEM((2, ROWS, D), BF),
            pltpu.VMEM((2, HALF, D), BF),
            pltpu.VMEM((2, ROWS, D), BF),
            pltpu.VMEM((ROWS, D), BF),
            pltpu.VMEM((2, ROWS, DH), BF),
            pltpu.VMEM((2, 2, ROWS, DH), BF),
            pltpu.VMEM((ROWS, DH), BF),
            pltpu.VMEM((ROWS, DH), BF),
            pltpu.VMEM((2, 4, 16, 64, CH), BF),
            pltpu.VMEM((2, 8, 64, CH), BF),
            pltpu.VMEM((4, 16, 64, CH), BF),
            pltpu.VMEM((4, 7, 2, 64, CH), BF),
            pltpu.VMEM((4, 64, CH), BF),
            pltpu.VMEM((4, 64, CH), F32),
            pltpu.VMEM((4, 64, CH), BF),
            dma((5,)),
            *[dma((10,))] * 2,
            *[dma((7,))] * 2,
            *[dma((1,))] * 2,
            *[dma((4,))] * 2,
            *[dma((4,))] * 2,
            *[dma((7,))] * 2,
            *[dma((10,))] * 2,
            *[dma((2,))] * 2,
            *[dma((4,))] * 2,
            *[dma((4, 7))] * 2,
            *[dma((4,))] * 2,
        ],
        compiler_params=pltpu.CompilerParams(
            collective_id=0, has_side_effects=True, vmem_limit_bytes=67043328
        ),
        name="hyena_block",
    )(
        tokens,
        gain.reshape(1, D),
        w_short,
        filters,
        skip.reshape(1, CH),
        jnp.transpose(w_in, (1, 0, 2)),
        w_out,
        cotangent,
    )
    results = (mixed, token_grad, gwi, gwo)
    mixed, token_grad, gwi, gwo = pl.pallas_call(
        place,
        out_shape=tuple(jax.ShapeDtypeStruct(r.shape, r.dtype) for r in results),
        in_specs=[vmem] * 4,
        out_specs=(vmem,) * 4,
        name="place",
    )(*results)
    return mixed, token_grad, jnp.transpose(gwi, (1, 0, 2)), gwo.T


def solution(mesh):
    return jax.shard_map(
        body,
        mesh=mesh,
        in_specs=(
            P(("dp", "tensor"), None),
            P(None),
            P(None, None, "tensor"),
            P(None, None, "tensor"),
            P("tensor", None),
            P("tensor"),
            P("tensor", None),
            P(("dp", "tensor"), None),
        ),
        out_specs=(
            P(("dp", "tensor"), None),
            P(("dp", "tensor"), None),
            P("dp", None, "tensor"),
            P("tensor", "dp"),
        ),
        check_vma=False,
    )
```

```python
import math

import jax
import jax.numpy as jnp
from jax import lax
from jax.experimental import pallas as pl
from jax.experimental.pallas import tpu as pltpu
from jax.sharding import PartitionSpec as P

MESH = pl.DeviceIdType.MESH
BF = jnp.bfloat16
F32 = jnp.float32
ROWS = 128
HALF = 64
DH = 1024
D = 2048
CH = 256
BLOCKS = 8
SEQ = 1024
NZ = 8
SCALE = 1.0 / math.sqrt(32768.0)
NT_DIMS = (((1,), (1,)), ((), ()))


def kernel(
    tok, gain, ws, filt, skip, w3_any, wo_any, cot_any,
    mixed_out, tig_out, gwi_out, gwo_out,
    bufa, chalf, mpart, nt, ct, win, wmine, wother, zbuf, qkv, ibuf, cbuf, gbuf, gother,
    ggmine, ggsend, ggother, gcb, gz, tfwd, tbwd, eye,
    q1, q2, q3, q4, q5, n3, n4, nsend, n5,
    grads, gout, cxb, rbuf, ysend, ykeep, yrecv,
    load_sem, n_s, n_r, c_s, c_r, w_s, w_r, ga_s, ga_r, gg_s, gg_r, m_s, m_r, t_s, t_r,
    go_s, go_r, cx_s, cx_r, ring_s, ring_r, y_s, y_r,
):
    t = lax.axis_index("tensor")
    d = lax.axis_index("dp")
    x, y = lax.div(t, 2), lax.rem(t, 2)
    z, yh, core = lax.div(d, 4), lax.rem(lax.div(d, 2), 2), lax.rem(d, 2)
    xp = {"tensor": lax.rem(x + 1, 4) * 2 + y}
    xm = {"tensor": lax.rem(x + 3, 4) * 2 + y}
    yp = {"tensor": x * 2 + 1 - y}
    zp = {"dp": lax.rem(z + 1, NZ) * 4 + yh * 2 + core}
    zm = {"dp": lax.rem(z + NZ - 1, NZ) * 4 + yh * 2 + core}
    outer = {"dp": z * 4 + (1 - yh) * 2 + core, "tensor": x * 2 + 1 - y}
    yhp = {"dp": z * 4 + (1 - yh) * 2 + core}
    cp = {"dp": z * 4 + yh * 2 + 1 - core}

    my_half = pl.ds(pl.multiple_of(y * DH, DH), DH)
    other_half = pl.ds(pl.multiple_of((1 - y) * DH, DH), DH)
    loads = [pltpu.make_async_copy(cot_any.at[:, my_half], chalf.at[0:ROWS], load_sem.at[0])]
    for j in range(3):
        loads.append(
            pltpu.make_async_copy(
                w3_any.at[j], win.at[:, j * CH : (j + 1) * CH], load_sem.at[1 + j]
            )
        )
    loads.append(pltpu.make_async_copy(wo_any.at[:, my_half], wmine, load_sem.at[4]))
    for c in loads:
        c.start()

    barrier = pltpu.get_barrier_semaphore()
    for dev in (xp, xm, yp, zp, zm, yhp, cp, outer):
        pl.semaphore_signal(barrier, inc=1, device_id=dev, device_id_type=MESH)

    def remote(src, dst, ss, rs, dev):
        return pltpu.make_async_remote_copy(
            src_ref=src, dst_ref=dst, send_sem=ss, recv_sem=rs, device_id=dev, device_id_type=MESH
        )

    def gather_copies(buf):
        def rows(slot, lo=0, n=ROWS):
            return buf.at[slot * ROWS + lo : slot * ROWS + lo + n]

        spec = [
            (rows(0), rows(1), yp),
            (rows(0, 0, HALF), rows(6, 0, HALF), xp),
            (rows(0, HALF, HALF), rows(6, HALF, HALF), xp),
            (rows(0, HALF, HALF), rows(2, HALF, HALF), xm),
            (rows(0, 0, HALF), rows(2, 0, HALF), xm),
            (rows(1), rows(7), xp),
            (rows(1), rows(3), xm),
            (rows(6, 0, HALF), rows(4, 0, HALF), xp),
            (rows(2, HALF, HALF), rows(4, HALF, HALF), xm),
            (rows(4), rows(5), yp),
        ]
        return [
            remote(s, e, n_s.at[i], n_r.at[i], dev) for i, (s, e, dev) in enumerate(spec)
        ]

    def half_copies():
        def rows(slot):
            return chalf.at[slot * ROWS : (slot + 1) * ROWS]

        spec = [
            (cot_any.at[:, other_half], rows(1), yp),
            (rows(0), rows(6), xp),
            (rows(1), rows(7), xp),
            (rows(1), rows(3), xm),
            (rows(0), rows(2), xm),
            (rows(6), rows(4), xp),
            (rows(3), rows(5), xm),
        ]
        return [remote(s, e, c_s.at[i], c_r.at[i], dev) for i, (s, e, dev) in enumerate(spec)]

    def mixed_copies():
        def rows(p, b):
            at = (2 * p + b) * ROWS
            return mpart.at[at : at + ROWS]

        spec = [
            (rows(2, 1), n3.at[0], xp),
            (rows(2, 0), n3.at[1], xm),
            (rows(1, 0), n4.at[0, 0], xp),
            (rows(1, 1), n4.at[0, 1], xp),
            (rows(3, 1), n4.at[1, 1], xm),
            (rows(3, 0), n4.at[1, 0], xm),
            (nsend, n5, yp),
        ]
        return [remote(s, e, m_s.at[i], m_r.at[i], dev) for i, (s, e, dev) in enumerate(spec)]

    def scatter_copies(buf):
        def rows(slot, lo=0, n=ROWS):
            return buf.at[slot * ROWS + lo : slot * ROWS + lo + n]

        lo, hi = slice(0, HALF), slice(HALF, ROWS)
        spec = [
            (rows(5), q1, yp),
            (rows(3), q2.at[0], xp),
            (rows(7), q2.at[1], xm),
            (rows(4, HALF, HALF), q3.at[0], xp),
            (rows(4, 0, HALF), q3.at[1], xm),
            (rows(2, 0, HALF), q4.at[0, lo], xp),
            (rows(2, HALF, HALF), q4.at[0, hi], xp),
            (rows(6, HALF, HALF), q4.at[1, hi], xm),
            (rows(6, 0, HALF), q4.at[1, lo], xm),
            (rows(1), q5, yp),
        ]
        return [
            remote(s, e, t_s.at[i], t_r.at[i], dev) for i, (s, e, dev) in enumerate(spec)
        ]

    def add_rows(buf, row, n, others):
        def step(i, _):
            at = pl.multiple_of(row + i * 16, 16)
            total = buf[pl.ds(at, 16), :].astype(F32)
            for o, shift in others:
                total = total + o[pl.ds(pl.multiple_of(shift + i * 16, 16), 16), :].astype(F32)
            buf[pl.ds(at, 16), :] = total.astype(BF)
            return 0

        lax.fori_loop(0, n // 16, step, 0, unroll=2)

    def add_far(buf, c):
        c[0].wait_recv()
        add_rows(buf, 4 * ROWS + HALF, HALF, [(q1, HALF)])
        c[3].start()
        add_rows(buf, 4 * ROWS, HALF, [(q1, 0)])
        c[4].start()

    def add_side(buf, c):
        c[1].wait_recv()
        c[2].wait_recv()
        add_rows(buf, 1 * ROWS, ROWS, [(q2.at[0], 0), (q2.at[1], 0)])
        c[9].start()

    def add_near(buf, c):
        c[3].wait_recv()
        add_rows(buf, 2 * ROWS + HALF, HALF, [(q3.at[0], 0)])
        c[6].start()
        c[4].wait_recv()
        add_rows(buf, 6 * ROWS, HALF, [(q3.at[1], 0)])
        c[8].start()

    def wait_last(c):
        for i in (5, 6, 7, 8, 9):
            c[i].wait_recv()

    def last_sum(buf, at):
        total = buf[pl.ds(at, 16), :].astype(F32)
        total = total + q4[0, pl.ds(at, 16), :].astype(F32)
        total = total + q4[1, pl.ds(at, 16), :].astype(F32)
        return total + q5[pl.ds(at, 16), :].astype(F32)

    def norm(i, _):
        at = pl.multiple_of(i * 16, 16)
        v = tok[pl.ds(at, 16), :].astype(F32)
        r = lax.rsqrt(jnp.mean(v * v, axis=-1, keepdims=True) + 1e-05)
        bufa[pl.ds(at, 16), :] = ((v * r) * gain[...]).astype(BF)
        return 0

    lax.fori_loop(0, ROWS // 16, norm, 0, unroll=4)

    pl.semaphore_wait(barrier, 8)
    ga = gather_copies(bufa)
    gc_ = half_copies()
    wx = remote(wo_any.at[:, other_half], wother, w_s.at[0], w_r.at[0], outer)
    for i in (0, 1, 3, 2, 4):
        ga[i].start()
    gc_[0].start()
    wx.start()

    eye[...] = (
        lax.broadcasted_iota(jnp.int32, (CH, CH), 0) == lax.broadcasted_iota(jnp.int32, (CH, CH), 1)
    ).astype(BF)
    for j in range(3):
        zbuf[j, 0:8, :] = jnp.zeros((8, CH), F32)
    ibuf[0:ROWS, :] = jnp.zeros((ROWS, CH), BF)
    gcb[SEQ : SEQ + ROWS, :] = jnp.zeros((ROWS, CH), BF)

    def tables(g, _):
        row = jnp.concatenate([filt[pl.ds(g, 1), :], jnp.zeros((1, ROWS), F32)], axis=1)
        band = pltpu.roll(
            jnp.broadcast_to(row, (ROWS, 2 * ROWS)), 0, 1, stride=1, stride_axis=0
        ).astype(BF)
        at = pl.multiple_of(g * ROWS, ROWS)
        tbwd[pl.ds(at, ROWS), :] = band
        unit = eye[0:ROWS, 0:ROWS]
        for h in range(2):
            tfwd[pl.ds(at, ROWS), (1 - h) * ROWS : (2 - h) * ROWS] = lax.dot_general(
                unit, band[:, h * ROWS : (h + 1) * ROWS], NT_DIMS, preferred_element_type=F32
            ).astype(BF)
        return 0

    lax.fori_loop(0, 16, tables, 0)

    def seq_rows(p):
        first = lax.rem(x + p, 4) * (2 * ROWS)
        return (
            pl.multiple_of(first, 2 * ROWS),
            pl.multiple_of(first + y * ROWS, ROWS),
            pl.multiple_of(first + (1 - y) * ROWS, ROWS),
        )

    def pair(p):
        return slice(p * 2 * ROWS, (p + 1) * 2 * ROWS)

    def project(xa):
        p = lax.rem(xa + 4 - x, 4)
        rows = pl.ds(pl.multiple_of(p * 2 * ROWS, 2 * ROWS), 2 * ROWS)
        r0, r1 = xa * 2 * ROWS + y * ROWS, xa * 2 * ROWS + (1 - y) * ROWS

        @pl.when(p == 1)
        def _():
            ga[6].wait_recv()

        @pl.when(p == 2)
        def _():
            ga[9].wait_recv()

        @pl.when(p == 3)
        def _():
            ga[5].wait_recv()

        for j in range(3):
            out = jnp.dot(bufa[rows, :], win[:, j * CH : (j + 1) * CH], preferred_element_type=F32)
            zbuf[j, pl.ds(pl.multiple_of(r0 + 8, 8), ROWS), :] = out[:ROWS]
            zbuf[j, pl.ds(pl.multiple_of(r1 + 8, 8), ROWS), :] = out[ROWS:]

    def turn(src, dst, p):
        _, r0, r1 = seq_rows(p)

        def step(i, _):
            at = pl.multiple_of(i * 256, 256)
            out = lax.dot_general(
                eye[...], src[pair(p), pl.ds(at, 256)], NT_DIMS, preferred_element_type=F32
            ).astype(BF)
            dst[pl.ds(at, 256), pl.ds(r0, ROWS)] = out[:, :ROWS]
            dst[pl.ds(at, 256), pl.ds(r1, ROWS)] = out[:, ROWS:]
            return 0

        lax.fori_loop(0, dst.shape[0] // 256, step, 0)

    def exchange(src, dst, ss, rs):
        out = []
        for p in range(4):
            rows = pl.ds(p * 2 * ROWS, 2 * ROWS)
            out.append(remote(src.at[rows], dst.at[rows], ss.at[p], rs.at[p], yp))
        return out

    gated_x = exchange(gbuf, gother, ga_s, ga_r)
    def gate_copy(xa):
        rows = pl.ds(pl.multiple_of(xa * 2 * ROWS, 2 * ROWS), 2 * ROWS)
        return remote(ggsend.at[rows], ggother.at[rows], gg_s.at[xa], gg_r.at[xa], yp)

    gate_x = [gate_copy(xa) for xa in range(4)]

    def back_gate(p):
        _, r0, r1 = seq_rows(p)
        for w, dst, kind in ((wother, ggsend, BF), (wmine, ggmine, F32)):
            out = lax.dot_general(
                chalf[pair(p), :], w[...], NT_DIMS, preferred_element_type=F32
            ).astype(kind)
            dst[pl.ds(r0, ROWS), :] = out[:ROWS]
            dst[pl.ds(r1, ROWS), :] = out[ROWS:]
        gate_copy(lax.rem(x + p, 4)).start()

    group = lax.shift_right_logical(lax.broadcasted_iota(jnp.int32, (ROWS, ROWS), 1), 4)

    def filtered(table, signal, base):
        outs = []
        for h in range(2):
            big = jnp.dot(
                table[h * 1024 : (h + 1) * 1024, :],
                signal[pl.ds(base, 2 * ROWS), h * ROWS : (h + 1) * ROWS],
                preferred_element_type=F32,
            )
            acc = big[0:ROWS]
            for g in range(1, 8):
                acc = jnp.where(group == g, big[g * ROWS : (g + 1) * ROWS], acc)
            outs.append(acc)
        return jnp.concatenate(outs, axis=1)

    def forward(b, _):
        base = pl.multiple_of(b * ROWS, ROWS)
        f = []
        for j in range(3):
            v = zbuf[j, pl.ds(base, ROWS + 8), :]
            f.append(
                ws[0, j : j + 1, :] * v[8 : 8 + ROWS]
                + ws[1, j : j + 1, :] * v[7 : 7 + ROWS]
                + ws[2, j : j + 1, :] * v[6 : 6 + ROWS]
            )
            qkv[j, pl.ds(base, ROWS), :] = f[j]
        inner = f[1] * f[2]
        ibuf[pl.ds(pl.multiple_of(base + ROWS, ROWS), ROWS), :] = inner.astype(BF)
        conv = filtered(tfwd, ibuf, base) + skip[...] * inner
        cbuf[pl.ds(base, ROWS), :] = conv
        gbuf[pl.ds(base, ROWS), :] = (qkv[0, pl.ds(base, ROWS), :] * conv).astype(BF)
        return 0

    def backward(i, _):
        base = pl.multiple_of((BLOCKS - 1 - i) * ROWS, ROWS)
        here = pl.ds(base, ROWS)
        gg = (ggmine[here, :] + ggother[here, :].astype(F32)).astype(BF).astype(F32)
        gc = gg * qkv[0, here, :]
        gcb[here, :] = gc.astype(BF)
        zbuf[0, here, :] = gg * cbuf[here, :]
        gi = filtered(tbwd, gcb, base) + skip[...] * gc
        zbuf[1, here, :] = gi * qkv[2, here, :]
        zbuf[2, here, :] = gi * qkv[1, here, :]
        for j in range(3):
            v = zbuf[j, pl.ds(base, ROWS + 8), :]
            gz[here, j * CH : (j + 1) * CH] = (
                ws[0, j : j + 1, :] * v[0:ROWS]
                + ws[1, j : j + 1, :] * v[1 : 1 + ROWS]
                + ws[2, j : j + 1, :] * v[2 : 2 + ROWS]
            ).astype(BF)
        return 0

    def mix(p):
        rows = pl.ds(seq_rows(p)[0], 2 * ROWS)

        def step(i, _):
            cols = pl.ds(pl.multiple_of(i * 512, 512), 512)
            out = jnp.dot(gbuf[rows, :], wmine[:, cols], preferred_element_type=F32)
            out = out + jnp.dot(gother[rows, :], wother[:, cols], preferred_element_type=F32)
            mpart[p * 2 * ROWS : (p + 1) * 2 * ROWS, cols] = out.astype(BF)
            return 0

        lax.fori_loop(0, DH // 512, step, 0)

    def back_norm(p):
        first, _, _ = seq_rows(p)
        at0 = pl.multiple_of(p * 2 * ROWS + y * ROWS, ROWS)
        at1 = pl.multiple_of(p * 2 * ROWS + (1 - y) * ROWS, ROWS)

        def step(i, _):
            cols = pl.ds(pl.multiple_of(i * 1024, 1024), 1024)
            out = lax.dot_general(
                gz[pl.ds(first, 2 * ROWS), :], win[cols, :], NT_DIMS, preferred_element_type=F32
            ).astype(BF)
            bufa[pl.ds(at0, ROWS), cols] = out[:ROWS]
            bufa[pl.ds(at1, ROWS), cols] = out[ROWS:]
            return 0

        lax.fori_loop(0, D // 1024, step, 0)

    def weight_grad(j, lhs, rhs, col):
        def step(i, _):
            out = jnp.dot(
                lhs[pl.ds(pl.multiple_of(i * 512, 512), 512), :],
                rhs[:, col : col + CH],
                preferred_element_type=F32,
            ).astype(BF)
            for h in range(4):
                for c in range(2):
                    r = (h * 2 + c) * 64
                    grads[c, j, i * 4 + h] = out[r : r + 64]
            return 0

        lax.fori_loop(0, NZ // 2, step, 0)

    def weight_grad_out():
        def step(i, _):
            lhs = ct[pl.ds(pl.multiple_of(i * 256, 256), 256), :]
            mine = jnp.dot(lhs, gbuf[...], preferred_element_type=F32).astype(BF)
            other = jnp.dot(lhs, gother[...], preferred_element_type=F32).astype(BF)
            for h in range(2):
                for c in range(2):
                    r = (h * 2 + c) * 64
                    grads[c, 3, y * 8 + i * 2 + h] = mine[r : r + 64]
                    gout[c, i * 2 + h] = other[r : r + 64]
            return 0

        lax.fori_loop(0, 4, step, 0)

    out_x = [
        remote(gout.at[core], grads.at[core, 3, pl.ds(y * 8, 8)], go_s.at[0], go_r.at[0], outer),
    ]
    out_cross = [
        remote(
            grads.at[1 - core, 3, pl.ds(y * 8, 8)], cxb.at[3, 0:8], cx_s.at[3], cx_r.at[3], cp
        ),
        remote(gout.at[1 - core], cxb.at[3, 8:16], go_s.at[1], go_r.at[1], cp),
    ]

    cross = [
        remote(grads.at[1 - core, j], cxb.at[j], cx_s.at[j], cx_r.at[j], cp) for j in range(3)
    ]
    hops = [{1: 4 - j % 2, -1: 3 + j % 2} for j in range(4)]
    ring = []
    for j in range(4):
        ring.append({})
        for s in (1, -1):
            n = hops[j][s]
            off = 0 if s == 1 else hops[j][1]
            ring[j][s] = []
            for i in range(n):
                zd = lax.rem(z + s * (n - i) + NZ, NZ)
                ring[j][s].append(
                    (
                        remote(
                            grads.at[core, j, pl.ds(zd * 2, 2)],
                            rbuf.at[j, off + i],
                            ring_s.at[j, off + i],
                            ring_r.at[j, off + i],
                            zp if s == 1 else zm,
                        ),
                        zd,
                        off + i,
                    )
                )

    def cross_add(j):
        cross[j].wait_recv()

        def step(i, _):
            grads[core, j, i] = (grads[core, j, i].astype(F32) + cxb[j, i].astype(F32)).astype(BF)
            return 0

        lax.fori_loop(0, 16, step, 0)

    def out_cross_add():
        out_cross[0].wait_recv()
        out_cross[1].wait_recv()

        def step(i, _):
            gout[core, i] = (gout[core, i].astype(F32) + cxb[3, 8 + i].astype(F32)).astype(BF)
            at = y * 8 + i
            grads[core, 3, at] = (grads[core, 3, at].astype(F32) + cxb[3, i].astype(F32)).astype(BF)
            return 0

        lax.fori_loop(0, 8, step, 0)

    def ring_round(j, i):
        for s in (1, -1):
            if i >= hops[j][s]:
                continue
            copy, zd, _ = ring[j][s][i]
            if i > 0:
                before, _, k = ring[j][s][i - 1]
                before.wait_recv()
                for h in range(2):
                    at = zd * 2 + h
                    grads[core, j, at] = (
                        grads[core, j, at].astype(F32) + rbuf[j, k, h].astype(F32)
                    ).astype(BF)
            copy.start()

    across = [remote(ysend.at[j], yrecv.at[j], y_s.at[j], y_r.at[j], yhp) for j in range(4)]

    def ring_end(j):
        ends = []
        for s in (1, -1):
            copy, _, k = ring[j][s][hops[j][s] - 1]
            copy.wait_recv()
            ends.append(k)

        def total(h):
            return (
                grads[core, j, z * 2 + h].astype(F32)
                + rbuf[j, ends[0], h].astype(F32)
                + rbuf[j, ends[1], h].astype(F32)
            )

        ysend[j] = total(1 - yh).astype(BF)
        across[j].start()
        ykeep[j] = total(yh)

    def add_cols(row, other):
        def step(i, _):
            at = pl.multiple_of(row + i * 32, 32)
            mpart[pl.ds(at, 32), :] = (
                mpart[pl.ds(at, 32), :].astype(F32)
                + other[pl.ds(pl.multiple_of(i * 32, 32), 32), :].astype(F32)
            ).astype(BF)
            return 0

        lax.fori_loop(0, ROWS // 32, step, 0)

    def mixed_sum(b, i):
        at = pl.ds(pl.multiple_of(b * ROWS + i * 32, 32), 32)
        here = pl.ds(pl.multiple_of(i * 32, 32), 32)
        return (
            mpart[at, :].astype(F32)
            + n4[0, b, here, :].astype(F32)
            + n4[1, b, here, :].astype(F32)
        ).astype(BF), here

    def mixed_other(i, _):
        out, here = mixed_sum(1 - y, i)
        nsend[here, :] = out
        return 0

    def mixed_mine(i, _):
        out, here = mixed_sum(y, i)
        mixed_out[here, my_half] = out
        return 0

    ga[1].wait_recv()
    ga[7].start()
    ga[3].wait_recv()
    ga[8].start()
    for c in loads:
        c.wait()
    ga[0].wait_recv()
    ga[5].start()
    ga[6].start()
    gc_[0].wait_recv()
    for i in (1, 3, 2, 4):
        gc_[i].start()
    ga[2].wait_recv()
    ga[4].wait_recv()
    ga[7].wait_recv()
    ga[8].wait_recv()
    ga[9].start()
    wx.wait_recv()
    turn(bufa, nt, 0)
    back_gate(0)
    turn(chalf, ct, 0)
    for p in range(4):
        project(p)
        lax.fori_loop(2 * p, 2 * p + 2, forward, 0)
        gated_x[p].start()
        if p == 2:
            gc_[1].wait_recv()
            gc_[5].start()
            gc_[3].wait_recv()
            gc_[6].start()
    for p in range(1, 4):
        turn(bufa, nt, p)
    gc_[4].wait_recv()
    back_gate(1)
    gc_[2].wait_recv()
    back_gate(3)
    turn(chalf, ct, 1)
    turn(chalf, ct, 3)
    for j in range(3):
        zbuf[j, SEQ : SEQ + 8, :] = jnp.zeros((8, CH), F32)
    gc_[5].wait_recv()
    gc_[6].wait_recv()
    back_gate(2)
    for p in range(4):
        gated_x[p].wait_recv()
    ma = mixed_copies()
    mix(2)
    ma[0].start()
    ma[1].start()
    mix(1)
    ma[2].start()
    mix(3)
    ma[4].start()
    mix(0)
    turn(chalf, ct, 2)
    weight_grad_out()
    for c in out_cross:
        c.start()
    for c in ga:
        c.wait_send()
    out_cross_add()
    out_x[0].start()
    for p in range(2):
        gate_x[3 - p].wait_recv()
        lax.fori_loop(2 * p, 2 * p + 2, backward, 0)
    ma[0].wait_recv()
    add_cols(3 * ROWS, n3.at[0])
    ma[3].start()
    ma[1].wait_recv()
    add_cols(6 * ROWS, n3.at[1])
    ma[5].start()
    for p in range(2, 4):
        gate_x[3 - p].wait_recv()
        lax.fori_loop(2 * p, 2 * p + 2, backward, 0)
    sb = scatter_copies(bufa)
    back_norm(2)
    sb[0].start()
    out_x[0].wait_recv()
    ring_round(3, 0)
    back_norm(1)
    sb[1].start()
    back_norm(3)
    sb[2].start()
    ring_round(3, 1)
    weight_grad(0, nt, gz, 0)
    cross[0].start()
    weight_grad(1, nt, gz, CH)
    cross[1].start()
    ring_round(3, 2)
    cross_add(0)
    ring_round(0, 0)
    weight_grad(2, nt, gz, 2 * CH)
    cross[2].start()
    cross_add(1)
    ring_round(1, 0)
    add_far(bufa, sb)
    sb[5].start()
    sb[7].start()
    ring_round(3, 3)
    cross_add(2)
    ring_round(2, 0)
    for i in (2, 3, 4, 5):
        ma[i].wait_recv()
    lax.fori_loop(0, 4, mixed_other, 0)
    ma[6].start()
    ring_round(0, 1)
    back_norm(0)
    add_side(bufa, sb)
    ring_round(1, 1)
    ring_end(3)
    ring_round(2, 1)
    ring_round(0, 2)
    ring_round(1, 2)
    add_near(bufa, sb)
    ring_round(2, 2)
    lax.fori_loop(0, 4, mixed_mine, 0)
    ring_round(0, 3)
    ring_round(1, 3)
    ring_round(2, 3)
    ma[6].wait_recv()
    mixed_out[:, other_half] = n5[...]
    for j in (0, 1, 2):
        ring_end(j)
    wait_last(sb)

    def finish_tokens(i, _):
        at = pl.multiple_of(i * 16, 16)
        v = tok[pl.ds(at, 16), :].astype(F32)
        r = lax.rsqrt(jnp.mean(v * v, axis=-1, keepdims=True) + 1e-05)
        xhat = v * r
        h = last_sum(bufa, at) * gain[...]
        tig_out[pl.ds(at, 16), :] = (
            r * (h - xhat * jnp.mean(h * xhat, axis=-1, keepdims=True))
        ).astype(BF)
        return 0

    lax.fori_loop(0, ROWS // 16, finish_tokens, 0, unroll=4)
    for j in (3, 0, 1, 2):
        across[j].wait_recv()
        out = (ykeep[j] + yrecv[j].astype(F32)) * SCALE
        if j == 3:
            gwo_out[...] = out
        else:
            gwi_out[j] = out
    for c in gc_ + [wx] + gated_x + gate_x + ma + sb + out_x + out_cross + cross + across:
        c.wait_send()
    for j in range(4):
        for s in (1, -1):
            for c, _, _ in ring[j][s]:
                c.wait_send()


def place(a, b, c, d, oa, ob, oc, od, va, vb, vc, vd, sem_in, sem_out):
    into = [
        pltpu.make_async_copy(src, mid, sem_in.at[i])
        for i, (src, mid) in enumerate(((a, va), (b, vb), (c, vc), (d, vd)))
    ]
    out = [
        pltpu.make_async_copy(mid, dst, sem_out.at[i])
        for i, (mid, dst) in enumerate(((va, oa), (vb, ob), (vc, oc), (vd, od)))
    ]
    for e in into:
        e.start()
    for e, f in zip(into, out):
        e.wait()
        f.start()
    for f in out:
        f.wait()


def body(tokens, gain, w_in, w_short, filters, skip, w_out, cotangent):
    vmem = pl.BlockSpec(memory_space=pltpu.VMEM)
    away = pl.BlockSpec(memory_space=pl.ANY)
    dma = pltpu.SemaphoreType.DMA
    mixed, token_grad, gwi, gwo = pl.pallas_call(
        kernel,
        out_shape=(
            jax.ShapeDtypeStruct((ROWS, D), BF),
            jax.ShapeDtypeStruct((ROWS, D), BF),
            jax.ShapeDtypeStruct((3, 64, CH), F32),
            jax.ShapeDtypeStruct((64, CH), F32),
        ),
        in_specs=[vmem] * 5 + [away] * 3,
        out_specs=(vmem,) * 4,
        scratch_shapes=[
            pltpu.VMEM((SEQ, D), BF),
            pltpu.VMEM((SEQ, DH), BF),
            pltpu.VMEM((SEQ, DH), BF),
            pltpu.VMEM((D, SEQ), BF),
            pltpu.VMEM((DH, SEQ), BF),
            pltpu.VMEM((D, 3 * CH), BF),
            pltpu.VMEM((CH, DH), BF),
            pltpu.VMEM((CH, DH), BF),
            pltpu.VMEM((3, SEQ + 8, CH), F32),
            pltpu.VMEM((3, SEQ, CH), F32),
            pltpu.VMEM((SEQ + ROWS, CH), BF),
            pltpu.VMEM((SEQ, CH), F32),
            pltpu.VMEM((SEQ, CH), BF),
            pltpu.VMEM((SEQ, CH), BF),
            pltpu.VMEM((SEQ, CH), F32),
            pltpu.VMEM((SEQ, CH), BF),
            pltpu.VMEM((SEQ, CH), BF),
            pltpu.VMEM((SEQ + ROWS, CH), BF),
            pltpu.VMEM((SEQ, 3 * CH), BF),
            pltpu.VMEM((2048, 256), BF),
            pltpu.VMEM((2048, 256), BF),
            pltpu.VMEM((CH, CH), BF),
            pltpu.VMEM((ROWS, D), BF),
            pltpu.VMEM((2, ROWS, D), BF),
            pltpu.VMEM((2, HALF, D), BF),
            pltpu.VMEM((2, ROWS, D), BF),
            pltpu.VMEM((ROWS, D), BF),
            pltpu.VMEM((2, ROWS, DH), BF),
            pltpu.VMEM((2, 2, ROWS, DH), BF),
            pltpu.VMEM((ROWS, DH), BF),
            pltpu.VMEM((ROWS, DH), BF),
            pltpu.VMEM((2, 4, 16, 64, CH), BF),
            pltpu.VMEM((2, 8, 64, CH), BF),
            pltpu.VMEM((4, 16, 64, CH), BF),
            pltpu.VMEM((4, 7, 2, 64, CH), BF),
            pltpu.VMEM((4, 64, CH), BF),
            pltpu.VMEM((4, 64, CH), F32),
            pltpu.VMEM((4, 64, CH), BF),
            dma((5,)),
            *[dma((10,))] * 2,
            *[dma((7,))] * 2,
            *[dma((1,))] * 2,
            *[dma((4,))] * 2,
            *[dma((4,))] * 2,
            *[dma((7,))] * 2,
            *[dma((10,))] * 2,
            *[dma((2,))] * 2,
            *[dma((4,))] * 2,
            *[dma((4, 7))] * 2,
            *[dma((4,))] * 2,
        ],
        compiler_params=pltpu.CompilerParams(
            collective_id=0, has_side_effects=True, vmem_limit_bytes=67043328
        ),
        name="hyena_block",
    )(
        tokens,
        gain.reshape(1, D),
        w_short,
        filters,
        skip.reshape(1, CH),
        jnp.transpose(w_in, (1, 0, 2)),
        w_out,
        cotangent,
    )
    results = (mixed, token_grad, gwi, gwo)
    mixed, token_grad, gwi, gwo = pl.pallas_call(
        place,
        out_shape=tuple(jax.ShapeDtypeStruct(r.shape, r.dtype) for r in results),
        in_specs=[away] * 4,
        out_specs=(away,) * 4,
        scratch_shapes=[pltpu.VMEM(r.shape, r.dtype) for r in results] + [dma((4,))] * 2,
        name="place",
    )(*results)
    return mixed, token_grad, jnp.transpose(gwi, (1, 0, 2)), gwo.T


def solution(mesh):
    return jax.shard_map(
        body,
        mesh=mesh,
        in_specs=(
            P(("dp", "tensor"), None),
            P(None),
            P(None, None, "tensor"),
            P(None, None, "tensor"),
            P("tensor", None),
            P("tensor"),
            P("tensor", None),
            P(("dp", "tensor"), None),
        ),
        out_specs=(
            P(("dp", "tensor"), None),
            P(("dp", "tensor"), None),
            P("dp", None, "tensor"),
            P("tensor", "dp"),
        ),
        check_vma=False,
    )
```

```python
import math

import jax
import jax.numpy as jnp
from jax import lax
from jax.experimental import pallas as pl
from jax.experimental.pallas import tpu as pltpu
from jax.sharding import PartitionSpec as P

MESH = pl.DeviceIdType.MESH
BF = jnp.bfloat16
F32 = jnp.float32
ROWS = 128
HALF = 64
DH = 1024
D = 2048
CH = 256
BLOCKS = 8
SEQ = 1024
NZ = 8
SCALE = 1.0 / math.sqrt(32768.0)
NT_DIMS = (((1,), (1,)), ((), ()))


def kernel(
    tok_any, gain_any, ws_any, filt_any, skip_any, w3_any, wo_any, cot_any,
    mixed_any, tig_any, gwi_any, gwo_any,
    tok, gain, ws, filt, skip, mixed_out, tig_out, gwi_out, gwo_out, wint,
    bufa, chalf, mpart, nt, ct, win, wmine, wother, zbuf, qkv, ibuf, cbuf, gbuf, gother,
    ggmine, ggsend, ggother, gcb, gz, tfwd, tbwd, eye,
    q1, q2, q3, q4, q5, n3, n4, nsend, n5,
    grads, gout, cxb, rbuf, ysend, ykeep, yrecv,
    load_sem, first_sem, store_sem, n_s, n_r, c_s, c_r, w_s, w_r, ga_s, ga_r, gg_s, gg_r, m_s, m_r, t_s, t_r,
    go_s, go_r, cx_s, cx_r, ring_s, ring_r, y_s, y_r,
):
    t = lax.axis_index("tensor")
    d = lax.axis_index("dp")
    x, y = lax.div(t, 2), lax.rem(t, 2)
    z, yh, core = lax.div(d, 4), lax.rem(lax.div(d, 2), 2), lax.rem(d, 2)
    xp = {"tensor": lax.rem(x + 1, 4) * 2 + y}
    xm = {"tensor": lax.rem(x + 3, 4) * 2 + y}
    yp = {"tensor": x * 2 + 1 - y}
    zp = {"dp": lax.rem(z + 1, NZ) * 4 + yh * 2 + core}
    zm = {"dp": lax.rem(z + NZ - 1, NZ) * 4 + yh * 2 + core}
    outer = {"dp": z * 4 + (1 - yh) * 2 + core, "tensor": x * 2 + 1 - y}
    yhp = {"dp": z * 4 + (1 - yh) * 2 + core}
    cp = {"dp": z * 4 + yh * 2 + 1 - core}

    barrier = pltpu.get_barrier_semaphore()
    for dev in (xp, xm, yp, zp, zm, yhp, cp, outer):
        pl.semaphore_signal(barrier, inc=1, device_id=dev, device_id_type=MESH)

    firsts = [
        pltpu.make_async_copy(src, dst, first_sem.at[i])
        for i, (src, dst) in enumerate(
            (
                (tok_any, tok),
                (gain_any, gain),
                (filt_any, filt),
                (ws_any, ws),
                (skip_any, skip),
            )
        )
    ]
    for c in firsts:
        c.start()
    my_half = pl.ds(pl.multiple_of(y * DH, DH), DH)
    other_half = pl.ds(pl.multiple_of((1 - y) * DH, DH), DH)
    loads = [pltpu.make_async_copy(cot_any.at[:, my_half], chalf.at[0:ROWS], load_sem.at[0])]
    for j in range(3):
        loads.append(
            pltpu.make_async_copy(
                w3_any.at[j], win.at[:, j * CH : (j + 1) * CH], load_sem.at[1 + j]
            )
        )
    loads.append(pltpu.make_async_copy(wo_any.at[:, my_half], wmine, load_sem.at[4]))
    for c in loads:
        c.start()

    def remote(src, dst, ss, rs, dev):
        return pltpu.make_async_remote_copy(
            src_ref=src, dst_ref=dst, send_sem=ss, recv_sem=rs, device_id=dev, device_id_type=MESH
        )

    def gather_copies(buf):
        def rows(slot, lo=0, n=ROWS):
            return buf.at[slot * ROWS + lo : slot * ROWS + lo + n]

        spec = [
            (rows(0), rows(1), yp),
            (rows(0, 0, HALF), rows(6, 0, HALF), xp),
            (rows(0, HALF, HALF), rows(6, HALF, HALF), xp),
            (rows(0, HALF, HALF), rows(2, HALF, HALF), xm),
            (rows(0, 0, HALF), rows(2, 0, HALF), xm),
            (rows(1), rows(7), xp),
            (rows(1), rows(3), xm),
            (rows(6, 0, HALF), rows(4, 0, HALF), xp),
            (rows(2, HALF, HALF), rows(4, HALF, HALF), xm),
            (rows(4), rows(5), yp),
        ]
        return [
            remote(s, e, n_s.at[i], n_r.at[i], dev) for i, (s, e, dev) in enumerate(spec)
        ]

    def half_copies():
        def rows(slot):
            return chalf.at[slot * ROWS : (slot + 1) * ROWS]

        spec = [
            (cot_any.at[:, other_half], rows(1), yp),
            (rows(0), rows(6), xp),
            (rows(1), rows(7), xp),
            (rows(1), rows(3), xm),
            (rows(0), rows(2), xm),
            (rows(6), rows(4), xp),
            (rows(3), rows(5), xm),
        ]
        return [remote(s, e, c_s.at[i], c_r.at[i], dev) for i, (s, e, dev) in enumerate(spec)]

    def mixed_copies():
        def rows(p, b):
            at = (2 * p + b) * ROWS
            return mpart.at[at : at + ROWS]

        spec = [
            (rows(2, 1), n3.at[0], xp),
            (rows(2, 0), n3.at[1], xm),
            (rows(1, 0), n4.at[0, 0], xp),
            (rows(1, 1), n4.at[0, 1], xp),
            (rows(3, 1), n4.at[1, 1], xm),
            (rows(3, 0), n4.at[1, 0], xm),
            (nsend, n5, yp),
        ]
        return [remote(s, e, m_s.at[i], m_r.at[i], dev) for i, (s, e, dev) in enumerate(spec)]

    def scatter_copies(buf):
        def rows(slot, lo=0, n=ROWS):
            return buf.at[slot * ROWS + lo : slot * ROWS + lo + n]

        lo, hi = slice(0, HALF), slice(HALF, ROWS)
        spec = [
            (rows(5), q1, yp),
            (rows(3), q2.at[0], xp),
            (rows(7), q2.at[1], xm),
            (rows(4, HALF, HALF), q3.at[0], xp),
            (rows(4, 0, HALF), q3.at[1], xm),
            (rows(2, 0, HALF), q4.at[0, lo], xp),
            (rows(2, HALF, HALF), q4.at[0, hi], xp),
            (rows(6, HALF, HALF), q4.at[1, hi], xm),
            (rows(6, 0, HALF), q4.at[1, lo], xm),
            (rows(1), q5, yp),
        ]
        return [
            remote(s, e, t_s.at[i], t_r.at[i], dev) for i, (s, e, dev) in enumerate(spec)
        ]

    def add_rows(buf, row, n, others):
        def step(i, _):
            at = pl.multiple_of(row + i * 16, 16)
            total = buf[pl.ds(at, 16), :].astype(F32)
            for o, shift in others:
                total = total + o[pl.ds(pl.multiple_of(shift + i * 16, 16), 16), :].astype(F32)
            buf[pl.ds(at, 16), :] = total.astype(BF)
            return 0

        lax.fori_loop(0, n // 16, step, 0, unroll=2)

    def add_far(buf, c):
        c[0].wait_recv()
        add_rows(buf, 4 * ROWS + HALF, HALF, [(q1, HALF)])
        c[3].start()
        add_rows(buf, 4 * ROWS, HALF, [(q1, 0)])
        c[4].start()

    def add_side(buf, c):
        c[1].wait_recv()
        c[2].wait_recv()
        add_rows(buf, 1 * ROWS, ROWS, [(q2.at[0], 0), (q2.at[1], 0)])
        c[9].start()

    def add_near(buf, c):
        c[3].wait_recv()
        add_rows(buf, 2 * ROWS + HALF, HALF, [(q3.at[0], 0)])
        c[6].start()
        c[4].wait_recv()
        add_rows(buf, 6 * ROWS, HALF, [(q3.at[1], 0)])
        c[8].start()

    def wait_last(c):
        for i in (5, 6, 7, 8, 9):
            c[i].wait_recv()

    def last_sum(buf, at):
        total = buf[pl.ds(at, 16), :].astype(F32)
        total = total + q4[0, pl.ds(at, 16), :].astype(F32)
        total = total + q4[1, pl.ds(at, 16), :].astype(F32)
        return total + q5[pl.ds(at, 16), :].astype(F32)

    def norm(i, _):
        at = pl.multiple_of(i * 16, 16)
        v = tok[pl.ds(at, 16), :].astype(F32)
        r = lax.rsqrt(jnp.mean(v * v, axis=-1, keepdims=True) + 1e-05)
        bufa[pl.ds(at, 16), :] = ((v * r) * gain[...]).astype(BF)
        return 0

    firsts[0].wait()
    firsts[1].wait()
    lax.fori_loop(0, ROWS // 16, norm, 0, unroll=4)

    pl.semaphore_wait(barrier, 8)
    ga = gather_copies(bufa)
    gc_ = half_copies()
    wx = remote(wo_any.at[:, other_half], wother, w_s.at[0], w_r.at[0], outer)
    for i in (0, 1, 3, 2, 4):
        ga[i].start()
    gc_[0].start()
    wx.start()

    eye[...] = (
        lax.broadcasted_iota(jnp.int32, (CH, CH), 0) == lax.broadcasted_iota(jnp.int32, (CH, CH), 1)
    ).astype(BF)
    for j in range(3):
        zbuf[j, 0:8, :] = jnp.zeros((8, CH), F32)
    ibuf[0:ROWS, :] = jnp.zeros((ROWS, CH), BF)
    gcb[SEQ : SEQ + ROWS, :] = jnp.zeros((ROWS, CH), BF)

    def tables(g, _):
        row = jnp.concatenate([filt[pl.ds(g, 1), :], jnp.zeros((1, ROWS), F32)], axis=1)
        band = pltpu.roll(
            jnp.broadcast_to(row, (ROWS, 2 * ROWS)), 0, 1, stride=1, stride_axis=0
        ).astype(BF)
        at = pl.multiple_of(g * ROWS, ROWS)
        tbwd[pl.ds(at, ROWS), :] = band
        unit = eye[0:ROWS, 0:ROWS]
        for h in range(2):
            tfwd[pl.ds(at, ROWS), (1 - h) * ROWS : (2 - h) * ROWS] = lax.dot_general(
                unit, band[:, h * ROWS : (h + 1) * ROWS], NT_DIMS, preferred_element_type=F32
            ).astype(BF)
        return 0

    for c in firsts[2:]:
        c.wait()
    lax.fori_loop(0, 16, tables, 0)

    def seq_rows(p):
        first = lax.rem(x + p, 4) * (2 * ROWS)
        return (
            pl.multiple_of(first, 2 * ROWS),
            pl.multiple_of(first + y * ROWS, ROWS),
            pl.multiple_of(first + (1 - y) * ROWS, ROWS),
        )

    def pair(p):
        return slice(p * 2 * ROWS, (p + 1) * 2 * ROWS)

    def project(xa):
        p = lax.rem(xa + 4 - x, 4)
        rows = pl.ds(pl.multiple_of(p * 2 * ROWS, 2 * ROWS), 2 * ROWS)
        r0, r1 = xa * 2 * ROWS + y * ROWS, xa * 2 * ROWS + (1 - y) * ROWS

        @pl.when(p == 1)
        def _():
            ga[6].wait_recv()

        @pl.when(p == 2)
        def _():
            ga[9].wait_recv()

        @pl.when(p == 3)
        def _():
            ga[5].wait_recv()

        for j in range(3):
            out = jnp.dot(bufa[rows, :], win[:, j * CH : (j + 1) * CH], preferred_element_type=F32)
            zbuf[j, pl.ds(pl.multiple_of(r0 + 8, 8), ROWS), :] = out[:ROWS]
            zbuf[j, pl.ds(pl.multiple_of(r1 + 8, 8), ROWS), :] = out[ROWS:]

    def turn(src, dst, p):
        _, r0, r1 = seq_rows(p)

        def step(i, _):
            at = pl.multiple_of(i * 256, 256)
            out = lax.dot_general(
                eye[...], src[pair(p), pl.ds(at, 256)], NT_DIMS, preferred_element_type=F32
            ).astype(BF)
            dst[pl.ds(at, 256), pl.ds(r0, ROWS)] = out[:, :ROWS]
            dst[pl.ds(at, 256), pl.ds(r1, ROWS)] = out[:, ROWS:]
            return 0

        lax.fori_loop(0, dst.shape[0] // 256, step, 0)

    def exchange(src, dst, ss, rs):
        out = []
        for p in range(4):
            rows = pl.ds(p * 2 * ROWS, 2 * ROWS)
            out.append(remote(src.at[rows], dst.at[rows], ss.at[p], rs.at[p], yp))
        return out

    gated_x = exchange(gbuf, gother, ga_s, ga_r)
    def gate_copy(xa):
        rows = pl.ds(pl.multiple_of(xa * 2 * ROWS, 2 * ROWS), 2 * ROWS)
        return remote(ggsend.at[rows], ggother.at[rows], gg_s.at[xa], gg_r.at[xa], yp)

    gate_x = [gate_copy(xa) for xa in range(4)]

    def back_gate(p):
        _, r0, r1 = seq_rows(p)
        for w, dst, kind in ((wother, ggsend, BF), (wmine, ggmine, F32)):
            out = lax.dot_general(
                chalf[pair(p), :], w[...], NT_DIMS, preferred_element_type=F32
            ).astype(kind)
            dst[pl.ds(r0, ROWS), :] = out[:ROWS]
            dst[pl.ds(r1, ROWS), :] = out[ROWS:]
        gate_copy(lax.rem(x + p, 4)).start()

    group = lax.shift_right_logical(lax.broadcasted_iota(jnp.int32, (ROWS, ROWS), 1), 4)

    def filtered(table, signal, base):
        outs = []
        for h in range(2):
            big = jnp.dot(
                table[h * 1024 : (h + 1) * 1024, :],
                signal[pl.ds(base, 2 * ROWS), h * ROWS : (h + 1) * ROWS],
                preferred_element_type=F32,
            )
            acc = big[0:ROWS]
            for g in range(1, 8):
                acc = jnp.where(group == g, big[g * ROWS : (g + 1) * ROWS], acc)
            outs.append(acc)
        return jnp.concatenate(outs, axis=1)

    def forward(b, _):
        base = pl.multiple_of(b * ROWS, ROWS)
        f = []
        for j in range(3):
            v = zbuf[j, pl.ds(base, ROWS + 8), :]
            f.append(
                ws[0, j : j + 1, :] * v[8 : 8 + ROWS]
                + ws[1, j : j + 1, :] * v[7 : 7 + ROWS]
                + ws[2, j : j + 1, :] * v[6 : 6 + ROWS]
            )
            qkv[j, pl.ds(base, ROWS), :] = f[j]
        inner = f[1] * f[2]
        ibuf[pl.ds(pl.multiple_of(base + ROWS, ROWS), ROWS), :] = inner.astype(BF)
        conv = filtered(tfwd, ibuf, base) + skip[...] * inner
        cbuf[pl.ds(base, ROWS), :] = conv
        gbuf[pl.ds(base, ROWS), :] = (qkv[0, pl.ds(base, ROWS), :] * conv).astype(BF)
        return 0

    def backward(i, _):
        base = pl.multiple_of((BLOCKS - 1 - i) * ROWS, ROWS)
        here = pl.ds(base, ROWS)
        gg = (ggmine[here, :] + ggother[here, :].astype(F32)).astype(BF).astype(F32)
        gc = gg * qkv[0, here, :]
        gcb[here, :] = gc.astype(BF)
        zbuf[0, here, :] = gg * cbuf[here, :]
        gi = filtered(tbwd, gcb, base) + skip[...] * gc
        zbuf[1, here, :] = gi * qkv[2, here, :]
        zbuf[2, here, :] = gi * qkv[1, here, :]
        for j in range(3):
            v = zbuf[j, pl.ds(base, ROWS + 8), :]
            gz[here, j * CH : (j + 1) * CH] = (
                ws[0, j : j + 1, :] * v[0:ROWS]
                + ws[1, j : j + 1, :] * v[1 : 1 + ROWS]
                + ws[2, j : j + 1, :] * v[2 : 2 + ROWS]
            ).astype(BF)
        return 0

    def mix(p):
        rows = pl.ds(seq_rows(p)[0], 2 * ROWS)

        def step(i, _):
            cols = pl.ds(pl.multiple_of(i * 512, 512), 512)
            out = jnp.dot(gbuf[rows, :], wmine[:, cols], preferred_element_type=F32)
            out = out + jnp.dot(gother[rows, :], wother[:, cols], preferred_element_type=F32)
            mpart[p * 2 * ROWS : (p + 1) * 2 * ROWS, cols] = out.astype(BF)
            return 0

        lax.fori_loop(0, DH // 512, step, 0)

    def turn_weights(i, _):
        at = pl.ds(pl.multiple_of(i * 256, 256), 256)
        for j in range(3):
            wint[j * CH : (j + 1) * CH, at] = lax.dot_general(
                eye[...], win[at, j * CH : (j + 1) * CH], NT_DIMS, preferred_element_type=F32
            ).astype(BF)
        return 0

    def back_norm(p):
        first, _, _ = seq_rows(p)
        at0 = pl.multiple_of(p * 2 * ROWS + y * ROWS, ROWS)
        at1 = pl.multiple_of(p * 2 * ROWS + (1 - y) * ROWS, ROWS)

        def step(i, _):
            cols = pl.ds(pl.multiple_of(i * 1024, 1024), 1024)
            out = jnp.dot(
                gz[pl.ds(first, 2 * ROWS), :], wint[:, cols], preferred_element_type=F32
            ).astype(BF)
            bufa[pl.ds(at0, ROWS), cols] = out[:ROWS]
            bufa[pl.ds(at1, ROWS), cols] = out[ROWS:]
            return 0

        lax.fori_loop(0, D // 1024, step, 0)

    def weight_grad(j, lhs, rhs, col):
        def step(i, _):
            out = jnp.dot(
                lhs[pl.ds(pl.multiple_of(i * 512, 512), 512), :],
                rhs[:, col : col + CH],
                preferred_element_type=F32,
            ).astype(BF)
            for h in range(4):
                for c in range(2):
                    r = (h * 2 + c) * 64
                    grads[c, j, i * 4 + h] = out[r : r + 64]
            return 0

        lax.fori_loop(0, NZ // 2, step, 0)

    def weight_grad_out():
        def step(i, _):
            lhs = ct[pl.ds(pl.multiple_of(i * 256, 256), 256), :]
            mine = jnp.dot(lhs, gbuf[...], preferred_element_type=F32).astype(BF)
            other = jnp.dot(lhs, gother[...], preferred_element_type=F32).astype(BF)
            for h in range(2):
                for c in range(2):
                    r = (h * 2 + c) * 64
                    grads[c, 3, y * 8 + i * 2 + h] = mine[r : r + 64]
                    gout[c, i * 2 + h] = other[r : r + 64]
            return 0

        lax.fori_loop(0, 4, step, 0)

    out_x = [
        remote(gout.at[core], grads.at[core, 3, pl.ds(y * 8, 8)], go_s.at[0], go_r.at[0], outer),
    ]
    out_cross = [
        remote(
            grads.at[1 - core, 3, pl.ds(y * 8, 8)], cxb.at[3, 0:8], cx_s.at[3], cx_r.at[3], cp
        ),
        remote(gout.at[1 - core], cxb.at[3, 8:16], go_s.at[1], go_r.at[1], cp),
    ]

    cross = [
        remote(grads.at[1 - core, j], cxb.at[j], cx_s.at[j], cx_r.at[j], cp) for j in range(3)
    ]
    hops = [{1: 4 - j % 2, -1: 3 + j % 2} for j in range(4)]
    ring = []
    for j in range(4):
        ring.append({})
        for s in (1, -1):
            n = hops[j][s]
            off = 0 if s == 1 else hops[j][1]
            ring[j][s] = []
            for i in range(n):
                zd = lax.rem(z + s * (n - i) + NZ, NZ)
                ring[j][s].append(
                    (
                        remote(
                            grads.at[core, j, pl.ds(zd * 2, 2)],
                            rbuf.at[j, off + i],
                            ring_s.at[j, off + i],
                            ring_r.at[j, off + i],
                            zp if s == 1 else zm,
                        ),
                        zd,
                        off + i,
                    )
                )

    def cross_add(j):
        cross[j].wait_recv()

        def step(i, _):
            grads[core, j, i] = (grads[core, j, i].astype(F32) + cxb[j, i].astype(F32)).astype(BF)
            return 0

        lax.fori_loop(0, 16, step, 0)

    def out_cross_add():
        out_cross[0].wait_recv()
        out_cross[1].wait_recv()

        def step(i, _):
            gout[core, i] = (gout[core, i].astype(F32) + cxb[3, 8 + i].astype(F32)).astype(BF)
            at = y * 8 + i
            grads[core, 3, at] = (grads[core, 3, at].astype(F32) + cxb[3, i].astype(F32)).astype(BF)
            return 0

        lax.fori_loop(0, 8, step, 0)

    def ring_round(j, i):
        for s in (1, -1):
            if i >= hops[j][s]:
                continue
            copy, zd, _ = ring[j][s][i]
            if i > 0:
                before, _, k = ring[j][s][i - 1]
                before.wait_recv()
                for h in range(2):
                    at = zd * 2 + h
                    grads[core, j, at] = (
                        grads[core, j, at].astype(F32) + rbuf[j, k, h].astype(F32)
                    ).astype(BF)
            copy.start()

    across = [remote(ysend.at[j], yrecv.at[j], y_s.at[j], y_r.at[j], yhp) for j in range(4)]

    def ring_end(j):
        ends = []
        for s in (1, -1):
            copy, _, k = ring[j][s][hops[j][s] - 1]
            copy.wait_recv()
            ends.append(k)

        def total(h):
            return (
                grads[core, j, z * 2 + h].astype(F32)
                + rbuf[j, ends[0], h].astype(F32)
                + rbuf[j, ends[1], h].astype(F32)
            )

        ysend[j] = total(1 - yh).astype(BF)
        across[j].start()
        ykeep[j] = total(yh)

    def add_cols(row, other):
        def step(i, _):
            at = pl.multiple_of(row + i * 32, 32)
            mpart[pl.ds(at, 32), :] = (
                mpart[pl.ds(at, 32), :].astype(F32)
                + other[pl.ds(pl.multiple_of(i * 32, 32), 32), :].astype(F32)
            ).astype(BF)
            return 0

        lax.fori_loop(0, ROWS // 32, step, 0)

    def mixed_sum(b, i):
        at = pl.ds(pl.multiple_of(b * ROWS + i * 32, 32), 32)
        here = pl.ds(pl.multiple_of(i * 32, 32), 32)
        return (
            mpart[at, :].astype(F32)
            + n4[0, b, here, :].astype(F32)
            + n4[1, b, here, :].astype(F32)
        ).astype(BF), here

    def mixed_other(i, _):
        out, here = mixed_sum(1 - y, i)
        nsend[here, :] = out
        return 0

    def mixed_mine(i, _):
        out, here = mixed_sum(y, i)
        mixed_out[here, my_half] = out
        return 0

    ga[1].wait_recv()
    ga[7].start()
    ga[3].wait_recv()
    ga[8].start()
    for c in loads:
        c.wait()
    ga[0].wait_recv()
    ga[5].start()
    ga[6].start()
    lax.fori_loop(0, D // 256, turn_weights, 0)
    gc_[0].wait_recv()
    for i in (1, 3, 2, 4):
        gc_[i].start()
    ga[2].wait_recv()
    ga[4].wait_recv()
    ga[7].wait_recv()
    ga[8].wait_recv()
    ga[9].start()
    wx.wait_recv()
    turn(bufa, nt, 0)
    back_gate(0)
    turn(chalf, ct, 0)
    for p in range(4):
        project(p)
        lax.fori_loop(2 * p, 2 * p + 2, forward, 0)
        gated_x[p].start()
        if p == 2:
            gc_[1].wait_recv()
            gc_[5].start()
            gc_[3].wait_recv()
            gc_[6].start()
    for p in range(1, 4):
        turn(bufa, nt, p)
    gc_[4].wait_recv()
    back_gate(1)
    gc_[2].wait_recv()
    back_gate(3)
    turn(chalf, ct, 1)
    turn(chalf, ct, 3)
    for j in range(3):
        zbuf[j, SEQ : SEQ + 8, :] = jnp.zeros((8, CH), F32)
    gc_[5].wait_recv()
    gc_[6].wait_recv()
    back_gate(2)
    for p in range(4):
        gated_x[p].wait_recv()
    ma = mixed_copies()
    mix(2)
    ma[0].start()
    ma[1].start()
    mix(1)
    ma[2].start()
    mix(3)
    ma[4].start()
    mix(0)
    turn(chalf, ct, 2)
    weight_grad_out()
    for c in out_cross:
        c.start()
    for c in ga:
        c.wait_send()
    out_cross_add()
    out_x[0].start()
    for p in range(2):
        gate_x[3 - p].wait_recv()
        lax.fori_loop(2 * p, 2 * p + 2, backward, 0)
    ma[0].wait_recv()
    add_cols(3 * ROWS, n3.at[0])
    ma[3].start()
    ma[1].wait_recv()
    add_cols(6 * ROWS, n3.at[1])
    ma[5].start()
    for p in range(2, 4):
        gate_x[3 - p].wait_recv()
        lax.fori_loop(2 * p, 2 * p + 2, backward, 0)
    sb = scatter_copies(bufa)
    back_norm(2)
    sb[0].start()
    out_x[0].wait_recv()
    ring_round(3, 0)
    back_norm(1)
    sb[1].start()
    back_norm(3)
    sb[2].start()
    ring_round(3, 1)
    weight_grad(0, nt, gz, 0)
    cross[0].start()
    weight_grad(1, nt, gz, CH)
    cross[1].start()
    for i in (2, 3, 4, 5):
        ma[i].wait_recv()
    lax.fori_loop(0, 4, mixed_other, 0)
    ma[6].start()
    ring_round(3, 2)
    cross_add(0)
    ring_round(0, 0)
    weight_grad(2, nt, gz, 2 * CH)
    cross[2].start()
    cross_add(1)
    ring_round(1, 0)
    back_norm(0)
    add_far(bufa, sb)
    sb[5].start()
    sb[7].start()
    ring_round(3, 3)
    cross_add(2)
    ring_round(2, 0)
    ring_round(0, 1)
    add_side(bufa, sb)
    ring_round(1, 1)
    ring_end(3)
    ring_round(2, 1)
    ring_round(0, 2)
    ring_round(1, 2)
    add_near(bufa, sb)
    ring_round(2, 2)
    lax.fori_loop(0, 4, mixed_mine, 0)
    ring_round(0, 3)
    ring_round(1, 3)
    ring_round(2, 3)
    ma[6].wait_recv()
    mixed_out[:, other_half] = n5[...]
    stores = [
        pltpu.make_async_copy(src, dst, store_sem.at[i])
        for i, (src, dst) in enumerate(
            (
                (mixed_out, mixed_any),
                (tig_out.at[0:HALF], tig_any.at[0:HALF]),
                (tig_out.at[HALF:ROWS], tig_any.at[HALF:ROWS]),
                (gwi_out, gwi_any),
                (gwo_out, gwo_any),
            )
        )
    ]
    stores[0].start()
    for j in (0, 1, 2):
        ring_end(j)
    wait_last(sb)

    def finish_tokens(i, _):
        at = pl.multiple_of(i * 16, 16)
        v = tok[pl.ds(at, 16), :].astype(F32)
        r = lax.rsqrt(jnp.mean(v * v, axis=-1, keepdims=True) + 1e-05)
        xhat = v * r
        h = last_sum(bufa, at) * gain[...]
        tig_out[pl.ds(at, 16), :] = (
            r * (h - xhat * jnp.mean(h * xhat, axis=-1, keepdims=True))
        ).astype(BF)
        return 0

    for h in range(2):
        lax.fori_loop(4 * h, 4 * h + 4, finish_tokens, 0, unroll=4)
        stores[1 + h].start()
    for j in (3, 0, 1, 2):
        across[j].wait_recv()
        out = (ykeep[j] + yrecv[j].astype(F32)) * SCALE
        if j == 3:
            gwo_out[...] = out
        else:
            gwi_out[j] = out
    stores[3].start()
    stores[4].start()
    for c in stores:
        c.wait()
    for c in gc_ + [wx] + gated_x + gate_x + ma + sb + out_x + out_cross + cross + across:
        c.wait_send()
    for j in range(4):
        for s in (1, -1):
            for c, _, _ in ring[j][s]:
                c.wait_send()


def place(a, b, c, d, oa, ob, oc, od, va, vb, vc, vd, sem_in, sem_out):
    into = [
        pltpu.make_async_copy(src, mid, sem_in.at[i])
        for i, (src, mid) in enumerate(((a, va), (b, vb), (c, vc), (d, vd)))
    ]
    out = [
        pltpu.make_async_copy(mid, dst, sem_out.at[i])
        for i, (mid, dst) in enumerate(((va, oa), (vb, ob), (vc, oc), (vd, od)))
    ]
    for e in into:
        e.start()
    for e, f in zip(into, out):
        e.wait()
        f.start()
    for f in out:
        f.wait()


def body(tokens, gain, w_in, w_short, filters, skip, w_out, cotangent):
    away = pl.BlockSpec(memory_space=pl.ANY)
    dma = pltpu.SemaphoreType.DMA
    mixed, token_grad, gwi, gwo = pl.pallas_call(
        kernel,
        out_shape=(
            jax.ShapeDtypeStruct((ROWS, D), BF),
            jax.ShapeDtypeStruct((ROWS, D), BF),
            jax.ShapeDtypeStruct((3, 64, CH), F32),
            jax.ShapeDtypeStruct((64, CH), F32),
        ),
        in_specs=[away] * 8,
        out_specs=(away,) * 4,
        scratch_shapes=[
            pltpu.VMEM((ROWS, D), BF),
            pltpu.VMEM((1, D), F32),
            pltpu.VMEM((3, 3, CH), F32),
            pltpu.VMEM((16, ROWS), F32),
            pltpu.VMEM((1, CH), F32),
            pltpu.VMEM((ROWS, D), BF),
            pltpu.VMEM((ROWS, D), BF),
            pltpu.VMEM((3, 64, CH), F32),
            pltpu.VMEM((64, CH), F32),
            pltpu.VMEM((3 * CH, D), BF),
            pltpu.VMEM((SEQ, D), BF),
            pltpu.VMEM((SEQ, DH), BF),
            pltpu.VMEM((SEQ, DH), BF),
            pltpu.VMEM((D, SEQ), BF),
            pltpu.VMEM((DH, SEQ), BF),
            pltpu.VMEM((D, 3 * CH), BF),
            pltpu.VMEM((CH, DH), BF),
            pltpu.VMEM((CH, DH), BF),
            pltpu.VMEM((3, SEQ + 8, CH), F32),
            pltpu.VMEM((3, SEQ, CH), F32),
            pltpu.VMEM((SEQ + ROWS, CH), BF),
            pltpu.VMEM((SEQ, CH), F32),
            pltpu.VMEM((SEQ, CH), BF),
            pltpu.VMEM((SEQ, CH), BF),
            pltpu.VMEM((SEQ, CH), F32),
            pltpu.VMEM((SEQ, CH), BF),
            pltpu.VMEM((SEQ, CH), BF),
            pltpu.VMEM((SEQ + ROWS, CH), BF),
            pltpu.VMEM((SEQ, 3 * CH), BF),
            pltpu.VMEM((2048, 256), BF),
            pltpu.VMEM((2048, 256), BF),
            pltpu.VMEM((CH, CH), BF),
            pltpu.VMEM((ROWS, D), BF),
            pltpu.VMEM((2, ROWS, D), BF),
            pltpu.VMEM((2, HALF, D), BF),
            pltpu.VMEM((2, ROWS, D), BF),
            pltpu.VMEM((ROWS, D), BF),
            pltpu.VMEM((2, ROWS, DH), BF),
            pltpu.VMEM((2, 2, ROWS, DH), BF),
            pltpu.VMEM((ROWS, DH), BF),
            pltpu.VMEM((ROWS, DH), BF),
            pltpu.VMEM((2, 4, 16, 64, CH), BF),
            pltpu.VMEM((2, 8, 64, CH), BF),
            pltpu.VMEM((4, 16, 64, CH), BF),
            pltpu.VMEM((4, 7, 2, 64, CH), BF),
            pltpu.VMEM((4, 64, CH), BF),
            pltpu.VMEM((4, 64, CH), F32),
            pltpu.VMEM((4, 64, CH), BF),
            dma((5,)),
            dma((5,)),
            dma((5,)),
            *[dma((10,))] * 2,
            *[dma((7,))] * 2,
            *[dma((1,))] * 2,
            *[dma((4,))] * 2,
            *[dma((4,))] * 2,
            *[dma((7,))] * 2,
            *[dma((10,))] * 2,
            *[dma((2,))] * 2,
            *[dma((4,))] * 2,
            *[dma((4, 7))] * 2,
            *[dma((4,))] * 2,
        ],
        compiler_params=pltpu.CompilerParams(
            collective_id=0, has_side_effects=True, vmem_limit_bytes=67043328
        ),
        name="hyena_block",
    )(
        tokens,
        gain.reshape(1, D),
        w_short,
        filters,
        skip.reshape(1, CH),
        jnp.transpose(w_in, (1, 0, 2)),
        w_out,
        cotangent,
    )
    results = (mixed, token_grad, gwi, gwo)
    mixed, token_grad, gwi, gwo = pl.pallas_call(
        place,
        out_shape=tuple(jax.ShapeDtypeStruct(r.shape, r.dtype) for r in results),
        in_specs=[away] * 4,
        out_specs=(away,) * 4,
        scratch_shapes=[pltpu.VMEM(r.shape, r.dtype) for r in results] + [dma((4,))] * 2,
        name="place",
    )(*results)
    return mixed, token_grad, jnp.transpose(gwi, (1, 0, 2)), gwo.T


def solution(mesh):
    return jax.shard_map(
        body,
        mesh=mesh,
        in_specs=(
            P(("dp", "tensor"), None),
            P(None),
            P(None, None, "tensor"),
            P(None, None, "tensor"),
            P("tensor", None),
            P("tensor"),
            P("tensor", None),
            P(("dp", "tensor"), None),
        ),
        out_specs=(
            P(("dp", "tensor"), None),
            P(("dp", "tensor"), None),
            P("dp", None, "tensor"),
            P("tensor", "dp"),
        ),
        check_vma=False,
    )
```

```python
import math

import jax
import jax.numpy as jnp
from jax import lax
from jax.experimental import pallas as pl
from jax.experimental.pallas import tpu as pltpu
from jax.sharding import PartitionSpec as P

MESH = pl.DeviceIdType.MESH
BF = jnp.bfloat16
F32 = jnp.float32
ROWS = 128
HALF = 64
DH = 1024
D = 2048
CH = 256
BLOCKS = 8
SEQ = 1024
NZ = 8
SCALE = 1.0 / math.sqrt(32768.0)
NT_DIMS = (((1,), (1,)), ((), ()))


def kernel(
    tok_any, gain_any, ws_any, filt_any, skip_any, w3_any, wo_any, cot_any,
    mixed_any, tig_any, gwi_any, gwo_any,
    tok, gain, ws, filt, skip, mixed_out, tig_out, gwi_out, gwo_out, wint,
    bufa, chalf, mpart, nt, ct, win, wmine, wother, zbuf, qkv, ibuf, cbuf, gbuf, gother,
    ggmine, ggsend, ggother, gcb, gz, tfwd, tbwd, eye,
    q1, q2, q3, q4, q5, n3, n4, nsend, n5,
    grads, gout, cxb, rbuf, ysend, ykeep, yrecv,
    load_sem, first_sem, store_sem, n_s, n_r, c_s, c_r, w_s, w_r, ga_s, ga_r, gg_s, gg_r, m_s, m_r, t_s, t_r,
    go_s, go_r, cx_s, cx_r, ring_s, ring_r, y_s, y_r,
):
    t = lax.axis_index("tensor")
    d = lax.axis_index("dp")
    x, y = lax.div(t, 2), lax.rem(t, 2)
    z, yh, core = lax.div(d, 4), lax.rem(lax.div(d, 2), 2), lax.rem(d, 2)
    xp = {"tensor": lax.rem(x + 1, 4) * 2 + y}
    xm = {"tensor": lax.rem(x + 3, 4) * 2 + y}
    yp = {"tensor": x * 2 + 1 - y}
    zp = {"dp": lax.rem(z + 1, NZ) * 4 + yh * 2 + core}
    zm = {"dp": lax.rem(z + NZ - 1, NZ) * 4 + yh * 2 + core}
    outer = {"dp": z * 4 + (1 - yh) * 2 + core, "tensor": x * 2 + 1 - y}
    yhp = {"dp": z * 4 + (1 - yh) * 2 + core}
    cp = {"dp": z * 4 + yh * 2 + 1 - core}

    barrier = pltpu.get_barrier_semaphore()
    for dev in (xp, xm, yp, zp, zm, yhp, cp, outer):
        pl.semaphore_signal(barrier, inc=1, device_id=dev, device_id_type=MESH)

    firsts = [
        pltpu.make_async_copy(src, dst, first_sem.at[i])
        for i, (src, dst) in enumerate(
            (
                (tok_any, tok),
                (gain_any, gain),
                (filt_any, filt),
                (ws_any, ws),
                (skip_any, skip),
            )
        )
    ]
    for c in firsts:
        c.start()
    my_half = pl.ds(pl.multiple_of(y * DH, DH), DH)
    other_half = pl.ds(pl.multiple_of((1 - y) * DH, DH), DH)
    loads = [pltpu.make_async_copy(cot_any.at[:, my_half], chalf.at[0:ROWS], load_sem.at[0])]
    for j in range(3):
        loads.append(
            pltpu.make_async_copy(
                w3_any.at[j], win.at[:, j * CH : (j + 1) * CH], load_sem.at[1 + j]
            )
        )
    loads.append(pltpu.make_async_copy(wo_any.at[:, my_half], wmine, load_sem.at[4]))
    for c in loads:
        c.start()

    def remote(src, dst, ss, rs, dev):
        return pltpu.make_async_remote_copy(
            src_ref=src, dst_ref=dst, send_sem=ss, recv_sem=rs, device_id=dev, device_id_type=MESH
        )

    def gather_copies(buf):
        def rows(slot, lo=0, n=ROWS):
            return buf.at[slot * ROWS + lo : slot * ROWS + lo + n]

        spec = [
            (rows(0), rows(1), yp),
            (rows(0, 0, HALF), rows(6, 0, HALF), xp),
            (rows(0, HALF, HALF), rows(6, HALF, HALF), xp),
            (rows(0, HALF, HALF), rows(2, HALF, HALF), xm),
            (rows(0, 0, HALF), rows(2, 0, HALF), xm),
            (rows(1), rows(7), xp),
            (rows(1), rows(3), xm),
            (rows(6, 0, HALF), rows(4, 0, HALF), xp),
            (rows(2, HALF, HALF), rows(4, HALF, HALF), xm),
            (rows(4), rows(5), yp),
        ]
        return [
            remote(s, e, n_s.at[i], n_r.at[i], dev) for i, (s, e, dev) in enumerate(spec)
        ]

    def half_copies():
        def rows(slot):
            return chalf.at[slot * ROWS : (slot + 1) * ROWS]

        spec = [
            (cot_any.at[:, other_half], rows(1), yp),
            (rows(0), rows(6), xp),
            (rows(1), rows(7), xp),
            (rows(1), rows(3), xm),
            (rows(0), rows(2), xm),
            (rows(6), rows(4), xp),
            (rows(3), rows(5), xm),
        ]
        return [remote(s, e, c_s.at[i], c_r.at[i], dev) for i, (s, e, dev) in enumerate(spec)]

    def mixed_copies():
        def rows(p, b):
            at = (2 * p + b) * ROWS
            return mpart.at[at : at + ROWS]

        spec = [
            (rows(2, 1), n3.at[0], xp),
            (rows(2, 0), n3.at[1], xm),
            (rows(1, 0), n4.at[0, 0], xp),
            (rows(1, 1), n4.at[0, 1], xp),
            (rows(3, 1), n4.at[1, 1], xm),
            (rows(3, 0), n4.at[1, 0], xm),
            (nsend, n5, yp),
        ]
        return [remote(s, e, m_s.at[i], m_r.at[i], dev) for i, (s, e, dev) in enumerate(spec)]

    def scatter_copies(buf):
        def rows(slot, lo=0, n=ROWS):
            return buf.at[slot * ROWS + lo : slot * ROWS + lo + n]

        lo, hi = slice(0, HALF), slice(HALF, ROWS)
        spec = [
            (rows(5), q1, yp),
            (rows(3), q2.at[0], xp),
            (rows(7), q2.at[1], xm),
            (rows(4, HALF, HALF), q3.at[0], xp),
            (rows(4, 0, HALF), q3.at[1], xm),
            (rows(2, 0, HALF), q4.at[0, lo], xp),
            (rows(2, HALF, HALF), q4.at[0, hi], xp),
            (rows(6, HALF, HALF), q4.at[1, hi], xm),
            (rows(6, 0, HALF), q4.at[1, lo], xm),
            (rows(1), q5, yp),
        ]
        return [
            remote(s, e, t_s.at[i], t_r.at[i], dev) for i, (s, e, dev) in enumerate(spec)
        ]

    def add_rows(buf, row, n, others):
        def step(i, _):
            at = pl.multiple_of(row + i * 16, 16)
            total = buf[pl.ds(at, 16), :].astype(F32)
            for o, shift in others:
                total = total + o[pl.ds(pl.multiple_of(shift + i * 16, 16), 16), :].astype(F32)
            buf[pl.ds(at, 16), :] = total.astype(BF)
            return 0

        lax.fori_loop(0, n // 16, step, 0, unroll=2)

    def add_far(buf, c):
        c[0].wait_recv()
        add_rows(buf, 4 * ROWS + HALF, HALF, [(q1, HALF)])
        c[3].start()
        add_rows(buf, 4 * ROWS, HALF, [(q1, 0)])
        c[4].start()

    def add_side(buf, c):
        c[1].wait_recv()
        c[2].wait_recv()
        add_rows(buf, 1 * ROWS, ROWS, [(q2.at[0], 0), (q2.at[1], 0)])
        c[9].start()

    def add_near(buf, c):
        c[3].wait_recv()
        add_rows(buf, 2 * ROWS + HALF, HALF, [(q3.at[0], 0)])
        c[6].start()
        c[4].wait_recv()
        add_rows(buf, 6 * ROWS, HALF, [(q3.at[1], 0)])
        c[8].start()

    def wait_last(c):
        for i in (5, 6, 7, 8, 9):
            c[i].wait_recv()

    def last_sum(buf, at):
        total = buf[pl.ds(at, 16), :].astype(F32)
        total = total + q4[0, pl.ds(at, 16), :].astype(F32)
        total = total + q4[1, pl.ds(at, 16), :].astype(F32)
        return total + q5[pl.ds(at, 16), :].astype(F32)

    def norm(i, _):
        at = pl.multiple_of(i * 16, 16)
        v = tok[pl.ds(at, 16), :].astype(F32)
        r = lax.rsqrt(jnp.mean(v * v, axis=-1, keepdims=True) + 1e-05)
        bufa[pl.ds(at, 16), :] = ((v * r) * gain[...]).astype(BF)
        return 0

    firsts[0].wait()
    firsts[1].wait()
    lax.fori_loop(0, ROWS // 16, norm, 0, unroll=4)

    pl.semaphore_wait(barrier, 8)
    ga = gather_copies(bufa)
    gc_ = half_copies()
    wx = remote(wo_any.at[:, other_half], wother, w_s.at[0], w_r.at[0], outer)
    for i in (0, 1, 3, 2, 4):
        ga[i].start()
    gc_[0].start()
    wx.start()

    eye[...] = (
        lax.broadcasted_iota(jnp.int32, (CH, CH), 0) == lax.broadcasted_iota(jnp.int32, (CH, CH), 1)
    ).astype(BF)
    for j in range(3):
        zbuf[j, 0:8, :] = jnp.zeros((8, CH), F32)
    ibuf[0:ROWS, :] = jnp.zeros((ROWS, CH), BF)
    gcb[SEQ : SEQ + ROWS, :] = jnp.zeros((ROWS, CH), BF)

    def tables(g, _):
        row = jnp.concatenate([filt[pl.ds(g, 1), :], jnp.zeros((1, ROWS), F32)], axis=1)
        band = pltpu.roll(
            jnp.broadcast_to(row, (ROWS, 2 * ROWS)), 0, 1, stride=1, stride_axis=0
        ).astype(BF)
        at = pl.multiple_of(g * ROWS, ROWS)
        tbwd[pl.ds(at, ROWS), :] = band
        unit = eye[0:ROWS, 0:ROWS]
        for h in range(2):
            tfwd[pl.ds(at, ROWS), (1 - h) * ROWS : (2 - h) * ROWS] = lax.dot_general(
                unit, band[:, h * ROWS : (h + 1) * ROWS], NT_DIMS, preferred_element_type=F32
            ).astype(BF)
        return 0

    for c in firsts[2:]:
        c.wait()
    lax.fori_loop(0, 16, tables, 0)

    def seq_rows(p):
        first = lax.rem(x + p, 4) * (2 * ROWS)
        return (
            pl.multiple_of(first, 2 * ROWS),
            pl.multiple_of(first + y * ROWS, ROWS),
            pl.multiple_of(first + (1 - y) * ROWS, ROWS),
        )

    def pair(p):
        return slice(p * 2 * ROWS, (p + 1) * 2 * ROWS)

    def project(xa):
        p = lax.rem(xa + 4 - x, 4)
        rows = pl.ds(pl.multiple_of(p * 2 * ROWS, 2 * ROWS), 2 * ROWS)
        r0, r1 = xa * 2 * ROWS + y * ROWS, xa * 2 * ROWS + (1 - y) * ROWS

        @pl.when(p == 1)
        def _():
            ga[6].wait_recv()

        @pl.when(p == 2)
        def _():
            ga[9].wait_recv()

        @pl.when(p == 3)
        def _():
            ga[5].wait_recv()

        for j in range(3):
            out = jnp.dot(bufa[rows, :], win[:, j * CH : (j + 1) * CH], preferred_element_type=F32)
            zbuf[j, pl.ds(pl.multiple_of(r0 + 8, 8), ROWS), :] = out[:ROWS]
            zbuf[j, pl.ds(pl.multiple_of(r1 + 8, 8), ROWS), :] = out[ROWS:]

    def turn(src, dst, p):
        _, r0, r1 = seq_rows(p)

        def step(i, _):
            at = pl.multiple_of(i * 256, 256)
            out = lax.dot_general(
                eye[...], src[pair(p), pl.ds(at, 256)], NT_DIMS, preferred_element_type=F32
            ).astype(BF)
            dst[pl.ds(at, 256), pl.ds(r0, ROWS)] = out[:, :ROWS]
            dst[pl.ds(at, 256), pl.ds(r1, ROWS)] = out[:, ROWS:]
            return 0

        lax.fori_loop(0, dst.shape[0] // 256, step, 0)

    def exchange(src, dst, ss, rs):
        out = []
        for p in range(4):
            rows = pl.ds(p * 2 * ROWS, 2 * ROWS)
            out.append(remote(src.at[rows], dst.at[rows], ss.at[p], rs.at[p], yp))
        return out

    gated_x = exchange(gbuf, gother, ga_s, ga_r)
    def gate_copy(xa):
        rows = pl.ds(pl.multiple_of(xa * 2 * ROWS, 2 * ROWS), 2 * ROWS)
        return remote(ggsend.at[rows], ggother.at[rows], gg_s.at[xa], gg_r.at[xa], yp)

    gate_x = [gate_copy(xa) for xa in range(4)]

    def back_gate(p):
        _, r0, r1 = seq_rows(p)
        for w, dst, kind in ((wother, ggsend, BF), (wmine, ggmine, F32)):
            out = lax.dot_general(
                chalf[pair(p), :], w[...], NT_DIMS, preferred_element_type=F32
            ).astype(kind)
            dst[pl.ds(r0, ROWS), :] = out[:ROWS]
            dst[pl.ds(r1, ROWS), :] = out[ROWS:]
        gate_copy(lax.rem(x + p, 4)).start()

    group = lax.shift_right_logical(lax.broadcasted_iota(jnp.int32, (ROWS, ROWS), 1), 4)

    def filtered(table, signal, base):
        outs = []
        for h in range(2):
            big = jnp.dot(
                table[h * 1024 : (h + 1) * 1024, :],
                signal[pl.ds(base, 2 * ROWS), h * ROWS : (h + 1) * ROWS],
                preferred_element_type=F32,
            )
            acc = big[0:ROWS]
            for g in range(1, 8):
                acc = jnp.where(group == g, big[g * ROWS : (g + 1) * ROWS], acc)
            outs.append(acc)
        return jnp.concatenate(outs, axis=1)

    def forward(b, _):
        base = pl.multiple_of(b * ROWS, ROWS)
        f = []
        for j in range(3):
            v = zbuf[j, pl.ds(base, ROWS + 8), :]
            f.append(
                ws[0, j : j + 1, :] * v[8 : 8 + ROWS]
                + ws[1, j : j + 1, :] * v[7 : 7 + ROWS]
                + ws[2, j : j + 1, :] * v[6 : 6 + ROWS]
            )
            qkv[j, pl.ds(base, ROWS), :] = f[j]
        inner = f[1] * f[2]
        ibuf[pl.ds(pl.multiple_of(base + ROWS, ROWS), ROWS), :] = inner.astype(BF)
        conv = filtered(tfwd, ibuf, base) + skip[...] * inner
        cbuf[pl.ds(base, ROWS), :] = conv
        gbuf[pl.ds(base, ROWS), :] = (qkv[0, pl.ds(base, ROWS), :] * conv).astype(BF)
        return 0

    def backward(i, _):
        base = pl.multiple_of((BLOCKS - 1 - i) * ROWS, ROWS)
        here = pl.ds(base, ROWS)
        gg = (ggmine[here, :] + ggother[here, :].astype(F32)).astype(BF).astype(F32)
        gc = gg * qkv[0, here, :]
        gcb[here, :] = gc.astype(BF)
        zbuf[0, here, :] = gg * cbuf[here, :]
        gi = filtered(tbwd, gcb, base) + skip[...] * gc
        zbuf[1, here, :] = gi * qkv[2, here, :]
        zbuf[2, here, :] = gi * qkv[1, here, :]
        for j in range(3):
            v = zbuf[j, pl.ds(base, ROWS + 8), :]
            gz[here, j * CH : (j + 1) * CH] = (
                ws[0, j : j + 1, :] * v[0:ROWS]
                + ws[1, j : j + 1, :] * v[1 : 1 + ROWS]
                + ws[2, j : j + 1, :] * v[2 : 2 + ROWS]
            ).astype(BF)
        return 0

    def mix(p):
        rows = pl.ds(seq_rows(p)[0], 2 * ROWS)

        def step(i, _):
            cols = pl.ds(pl.multiple_of(i * 512, 512), 512)
            out = jnp.dot(gbuf[rows, :], wmine[:, cols], preferred_element_type=F32)
            out = out + jnp.dot(gother[rows, :], wother[:, cols], preferred_element_type=F32)
            mpart[p * 2 * ROWS : (p + 1) * 2 * ROWS, cols] = out.astype(BF)
            return 0

        lax.fori_loop(0, DH // 512, step, 0)

    def turn_weights(i, _):
        at = pl.ds(pl.multiple_of(i * 256, 256), 256)
        for j in range(3):
            wint[j * CH : (j + 1) * CH, at] = lax.dot_general(
                eye[...], win[at, j * CH : (j + 1) * CH], NT_DIMS, preferred_element_type=F32
            ).astype(BF)
        return 0

    def back_norm(p):
        first, _, _ = seq_rows(p)
        at0 = pl.multiple_of(p * 2 * ROWS + y * ROWS, ROWS)
        at1 = pl.multiple_of(p * 2 * ROWS + (1 - y) * ROWS, ROWS)

        def step(i, _):
            cols = pl.ds(pl.multiple_of(i * 1024, 1024), 1024)
            out = jnp.dot(
                gz[pl.ds(first, 2 * ROWS), :], wint[:, cols], preferred_element_type=F32
            ).astype(BF)
            bufa[pl.ds(at0, ROWS), cols] = out[:ROWS]
            bufa[pl.ds(at1, ROWS), cols] = out[ROWS:]
            return 0

        lax.fori_loop(0, D // 1024, step, 0)

    def weight_grad(j, lhs, rhs, col):
        def step(i, _):
            out = jnp.dot(
                lhs[pl.ds(pl.multiple_of(i * 512, 512), 512), :],
                rhs[:, col : col + CH],
                preferred_element_type=F32,
            ).astype(BF)
            for h in range(4):
                for c in range(2):
                    r = (h * 2 + c) * 64
                    grads[c, j, i * 4 + h] = out[r : r + 64]
            return 0

        lax.fori_loop(0, NZ // 2, step, 0)

    def weight_grad_out():
        def step(i, _):
            lhs = ct[pl.ds(pl.multiple_of(i * 256, 256), 256), :]
            mine = jnp.dot(lhs, gbuf[...], preferred_element_type=F32).astype(BF)
            other = jnp.dot(lhs, gother[...], preferred_element_type=F32).astype(BF)
            for h in range(2):
                for c in range(2):
                    r = (h * 2 + c) * 64
                    grads[c, 3, y * 8 + i * 2 + h] = mine[r : r + 64]
                    gout[c, i * 2 + h] = other[r : r + 64]
            return 0

        lax.fori_loop(0, 4, step, 0)

    out_x = [
        remote(gout.at[core], grads.at[core, 3, pl.ds(y * 8, 8)], go_s.at[0], go_r.at[0], outer),
    ]
    out_cross = [
        remote(
            grads.at[1 - core, 3, pl.ds(y * 8, 8)], cxb.at[3, 0:8], cx_s.at[3], cx_r.at[3], cp
        ),
        remote(gout.at[1 - core], cxb.at[3, 8:16], go_s.at[1], go_r.at[1], cp),
    ]

    cross = [
        remote(grads.at[1 - core, j], cxb.at[j], cx_s.at[j], cx_r.at[j], cp) for j in range(3)
    ]
    hops = [{1: 4 - j % 2, -1: 3 + j % 2} for j in range(4)]
    ring = []
    for j in range(4):
        ring.append({})
        for s in (1, -1):
            n = hops[j][s]
            off = 0 if s == 1 else hops[j][1]
            ring[j][s] = []
            for i in range(n):
                zd = lax.rem(z + s * (n - i) + NZ, NZ)
                ring[j][s].append(
                    (
                        remote(
                            grads.at[core, j, pl.ds(zd * 2, 2)],
                            rbuf.at[j, off + i],
                            ring_s.at[j, off + i],
                            ring_r.at[j, off + i],
                            zp if s == 1 else zm,
                        ),
                        zd,
                        off + i,
                    )
                )

    def cross_add(j):
        cross[j].wait_recv()

        def step(i, _):
            grads[core, j, i] = (grads[core, j, i].astype(F32) + cxb[j, i].astype(F32)).astype(BF)
            return 0

        lax.fori_loop(0, 16, step, 0)

    def out_cross_add():
        out_cross[0].wait_recv()
        out_cross[1].wait_recv()

        def step(i, _):
            gout[core, i] = (gout[core, i].astype(F32) + cxb[3, 8 + i].astype(F32)).astype(BF)
            at = y * 8 + i
            grads[core, 3, at] = (grads[core, 3, at].astype(F32) + cxb[3, i].astype(F32)).astype(BF)
            return 0

        lax.fori_loop(0, 8, step, 0)

    def ring_round(j, i):
        for s in (1, -1):
            if i >= hops[j][s]:
                continue
            copy, zd, _ = ring[j][s][i]
            if i > 0:
                before, _, k = ring[j][s][i - 1]
                before.wait_recv()
                for h in range(2):
                    at = zd * 2 + h
                    grads[core, j, at] = (
                        grads[core, j, at].astype(F32) + rbuf[j, k, h].astype(F32)
                    ).astype(BF)
            copy.start()

    across = [remote(ysend.at[j], yrecv.at[j], y_s.at[j], y_r.at[j], yhp) for j in range(4)]

    def ring_end(j):
        ends = []
        for s in (1, -1):
            copy, _, k = ring[j][s][hops[j][s] - 1]
            copy.wait_recv()
            ends.append(k)

        def total(h):
            return (
                grads[core, j, z * 2 + h].astype(F32)
                + rbuf[j, ends[0], h].astype(F32)
                + rbuf[j, ends[1], h].astype(F32)
            )

        ysend[j] = total(1 - yh).astype(BF)
        across[j].start()
        ykeep[j] = total(yh)

    def add_cols(row, other):
        def step(i, _):
            at = pl.multiple_of(row + i * 32, 32)
            mpart[pl.ds(at, 32), :] = (
                mpart[pl.ds(at, 32), :].astype(F32)
                + other[pl.ds(pl.multiple_of(i * 32, 32), 32), :].astype(F32)
            ).astype(BF)
            return 0

        lax.fori_loop(0, ROWS // 32, step, 0)

    def mixed_sum(b, i):
        at = pl.ds(pl.multiple_of(b * ROWS + i * 32, 32), 32)
        here = pl.ds(pl.multiple_of(i * 32, 32), 32)
        return (
            mpart[at, :].astype(F32)
            + n4[0, b, here, :].astype(F32)
            + n4[1, b, here, :].astype(F32)
        ).astype(BF), here

    def mixed_other(i, _):
        out, here = mixed_sum(1 - y, i)
        nsend[here, :] = out
        return 0

    def mixed_mine(i, _):
        out, here = mixed_sum(y, i)
        mixed_out[here, my_half] = out
        return 0

    ga[1].wait_recv()
    ga[7].start()
    ga[3].wait_recv()
    ga[8].start()
    for c in loads:
        c.wait()
    ga[0].wait_recv()
    ga[5].start()
    ga[6].start()
    lax.fori_loop(0, D // 256, turn_weights, 0)
    gc_[0].wait_recv()
    for i in (1, 3, 2, 4):
        gc_[i].start()
    ga[2].wait_recv()
    ga[4].wait_recv()
    ga[7].wait_recv()
    ga[8].wait_recv()
    ga[9].start()
    wx.wait_recv()
    turn(bufa, nt, 0)
    back_gate(0)
    turn(chalf, ct, 0)
    for p in range(4):
        project(p)
        lax.fori_loop(2 * p, 2 * p + 2, forward, 0)
        gated_x[p].start()
        if p == 2:
            gc_[1].wait_recv()
            gc_[5].start()
            gc_[3].wait_recv()
            gc_[6].start()
    for p in range(1, 4):
        turn(bufa, nt, p)
    gc_[4].wait_recv()
    back_gate(1)
    gc_[2].wait_recv()
    back_gate(3)
    turn(chalf, ct, 1)
    turn(chalf, ct, 3)
    for j in range(3):
        zbuf[j, SEQ : SEQ + 8, :] = jnp.zeros((8, CH), F32)
    gc_[5].wait_recv()
    gc_[6].wait_recv()
    back_gate(2)
    for p in range(4):
        gated_x[p].wait_recv()
    ma = mixed_copies()
    mix(2)
    ma[0].start()
    ma[1].start()
    mix(1)
    ma[2].start()
    mix(3)
    ma[4].start()
    mix(0)
    turn(chalf, ct, 2)
    weight_grad_out()
    for c in out_cross:
        c.start()
    for c in ga:
        c.wait_send()
    out_cross_add()
    out_x[0].start()
    for p in range(2):
        gate_x[3 - p].wait_recv()
        lax.fori_loop(2 * p, 2 * p + 2, backward, 0)
    ma[0].wait_recv()
    add_cols(3 * ROWS, n3.at[0])
    ma[3].start()
    ma[1].wait_recv()
    add_cols(6 * ROWS, n3.at[1])
    ma[5].start()
    for p in range(2, 4):
        gate_x[3 - p].wait_recv()
        lax.fori_loop(2 * p, 2 * p + 2, backward, 0)
    sb = scatter_copies(bufa)
    back_norm(2)
    sb[0].start()
    out_x[0].wait_recv()
    ring_round(3, 0)
    back_norm(1)
    sb[1].start()
    back_norm(3)
    sb[2].start()
    ring_round(3, 1)
    weight_grad(0, nt, gz, 0)
    cross[0].start()
    weight_grad(1, nt, gz, CH)
    cross[1].start()
    for i in (2, 3, 4, 5):
        ma[i].wait_recv()
    lax.fori_loop(0, 4, mixed_other, 0)
    ma[6].start()
    ring_round(3, 2)
    cross_add(0)
    ring_round(0, 0)
    weight_grad(2, nt, gz, 2 * CH)
    cross[2].start()
    cross_add(1)
    ring_round(1, 0)
    back_norm(0)
    add_far(bufa, sb)
    sb[5].start()
    sb[7].start()
    add_side(bufa, sb)
    ring_round(3, 3)
    cross_add(2)
    ring_round(2, 0)
    ring_round(0, 1)
    ring_round(1, 1)
    ring_end(3)
    ring_round(2, 1)
    ring_round(0, 2)
    ring_round(1, 2)
    add_near(bufa, sb)
    ring_round(2, 2)
    lax.fori_loop(0, 4, mixed_mine, 0)
    ring_round(0, 3)
    ring_round(1, 3)
    ring_round(2, 3)
    ma[6].wait_recv()
    mixed_out[:, other_half] = n5[...]
    stores = [
        pltpu.make_async_copy(src, dst, store_sem.at[i])
        for i, (src, dst) in enumerate(
            (
                (mixed_out, mixed_any),
                (tig_out.at[0:HALF], tig_any.at[0:HALF]),
                (tig_out.at[HALF:ROWS], tig_any.at[HALF:ROWS]),
                (gwi_out, gwi_any),
                (gwo_out, gwo_any),
            )
        )
    ]
    stores[0].start()
    for j in (0, 1, 2):
        ring_end(j)
    wait_last(sb)

    def finish_tokens(i, _):
        at = pl.multiple_of(i * 16, 16)
        v = tok[pl.ds(at, 16), :].astype(F32)
        r = lax.rsqrt(jnp.mean(v * v, axis=-1, keepdims=True) + 1e-05)
        xhat = v * r
        h = last_sum(bufa, at) * gain[...]
        tig_out[pl.ds(at, 16), :] = (
            r * (h - xhat * jnp.mean(h * xhat, axis=-1, keepdims=True))
        ).astype(BF)
        return 0

    for h in range(2):
        lax.fori_loop(4 * h, 4 * h + 4, finish_tokens, 0, unroll=4)
        stores[1 + h].start()
    for j in (3, 0, 1, 2):
        across[j].wait_recv()
        out = (ykeep[j] + yrecv[j].astype(F32)) * SCALE
        if j == 3:
            gwo_out[...] = out
        else:
            gwi_out[j] = out
    stores[3].start()
    stores[4].start()
    for c in stores:
        c.wait()
    for c in gc_ + [wx] + gated_x + gate_x + ma + sb + out_x + out_cross + cross + across:
        c.wait_send()
    for j in range(4):
        for s in (1, -1):
            for c, _, _ in ring[j][s]:
                c.wait_send()


def place(a, b, c, d, oa, ob, oc, od, va, vb, vc, vd, sem_in, sem_out):
    into = [
        pltpu.make_async_copy(src, mid, sem_in.at[i])
        for i, (src, mid) in enumerate(((a, va), (b, vb), (c, vc), (d, vd)))
    ]
    out = [
        pltpu.make_async_copy(mid, dst, sem_out.at[i])
        for i, (mid, dst) in enumerate(((va, oa), (vb, ob), (vc, oc), (vd, od)))
    ]
    for e in into:
        e.start()
    for e, f in zip(into, out):
        e.wait()
        f.start()
    for f in out:
        f.wait()


def body(tokens, gain, w_in, w_short, filters, skip, w_out, cotangent):
    away = pl.BlockSpec(memory_space=pl.ANY)
    dma = pltpu.SemaphoreType.DMA
    mixed, token_grad, gwi, gwo = pl.pallas_call(
        kernel,
        out_shape=(
            jax.ShapeDtypeStruct((ROWS, D), BF),
            jax.ShapeDtypeStruct((ROWS, D), BF),
            jax.ShapeDtypeStruct((3, 64, CH), F32),
            jax.ShapeDtypeStruct((64, CH), F32),
        ),
        in_specs=[away] * 8,
        out_specs=(away,) * 4,
        scratch_shapes=[
            pltpu.VMEM((ROWS, D), BF),
            pltpu.VMEM((1, D), F32),
            pltpu.VMEM((3, 3, CH), F32),
            pltpu.VMEM((16, ROWS), F32),
            pltpu.VMEM((1, CH), F32),
            pltpu.VMEM((ROWS, D), BF),
            pltpu.VMEM((ROWS, D), BF),
            pltpu.VMEM((3, 64, CH), F32),
            pltpu.VMEM((64, CH), F32),
            pltpu.VMEM((3 * CH, D), BF),
            pltpu.VMEM((SEQ, D), BF),
            pltpu.VMEM((SEQ, DH), BF),
            pltpu.VMEM((SEQ, DH), BF),
            pltpu.VMEM((D, SEQ), BF),
            pltpu.VMEM((DH, SEQ), BF),
            pltpu.VMEM((D, 3 * CH), BF),
            pltpu.VMEM((CH, DH), BF),
            pltpu.VMEM((CH, DH), BF),
            pltpu.VMEM((3, SEQ + 8, CH), F32),
            pltpu.VMEM((3, SEQ, CH), F32),
            pltpu.VMEM((SEQ + ROWS, CH), BF),
            pltpu.VMEM((SEQ, CH), F32),
            pltpu.VMEM((SEQ, CH), BF),
            pltpu.VMEM((SEQ, CH), BF),
            pltpu.VMEM((SEQ, CH), F32),
            pltpu.VMEM((SEQ, CH), BF),
            pltpu.VMEM((SEQ, CH), BF),
            pltpu.VMEM((SEQ + ROWS, CH), BF),
            pltpu.VMEM((SEQ, 3 * CH), BF),
            pltpu.VMEM((2048, 256), BF),
            pltpu.VMEM((2048, 256), BF),
            pltpu.VMEM((CH, CH), BF),
            pltpu.VMEM((ROWS, D), BF),
            pltpu.VMEM((2, ROWS, D), BF),
            pltpu.VMEM((2, HALF, D), BF),
            pltpu.VMEM((2, ROWS, D), BF),
            pltpu.VMEM((ROWS, D), BF),
            pltpu.VMEM((2, ROWS, DH), BF),
            pltpu.VMEM((2, 2, ROWS, DH), BF),
            pltpu.VMEM((ROWS, DH), BF),
            pltpu.VMEM((ROWS, DH), BF),
            pltpu.VMEM((2, 4, 16, 64, CH), BF),
            pltpu.VMEM((2, 8, 64, CH), BF),
            pltpu.VMEM((4, 16, 64, CH), BF),
            pltpu.VMEM((4, 7, 2, 64, CH), BF),
            pltpu.VMEM((4, 64, CH), BF),
            pltpu.VMEM((4, 64, CH), F32),
            pltpu.VMEM((4, 64, CH), BF),
            dma((5,)),
            dma((5,)),
            dma((5,)),
            *[dma((10,))] * 2,
            *[dma((7,))] * 2,
            *[dma((1,))] * 2,
            *[dma((4,))] * 2,
            *[dma((4,))] * 2,
            *[dma((7,))] * 2,
            *[dma((10,))] * 2,
            *[dma((2,))] * 2,
            *[dma((4,))] * 2,
            *[dma((4, 7))] * 2,
            *[dma((4,))] * 2,
        ],
        compiler_params=pltpu.CompilerParams(
            collective_id=0, has_side_effects=True, vmem_limit_bytes=67043328
        ),
        name="hyena_block",
    )(
        tokens,
        gain.reshape(1, D),
        w_short,
        filters,
        skip.reshape(1, CH),
        jnp.transpose(w_in, (1, 0, 2)),
        w_out,
        cotangent,
    )
    results = (mixed, token_grad, gwi, gwo)
    mixed, token_grad, gwi, gwo = pl.pallas_call(
        place,
        out_shape=tuple(jax.ShapeDtypeStruct(r.shape, r.dtype) for r in results),
        in_specs=[away] * 4,
        out_specs=(away,) * 4,
        scratch_shapes=[pltpu.VMEM(r.shape, r.dtype) for r in results] + [dma((4,))] * 2,
        name="place",
    )(*results)
    return mixed, token_grad, jnp.transpose(gwi, (1, 0, 2)), gwo.T


def solution(mesh):
    return jax.shard_map(
        body,
        mesh=mesh,
        in_specs=(
            P(("dp", "tensor"), None),
            P(None),
            P(None, None, "tensor"),
            P(None, None, "tensor"),
            P("tensor", None),
            P("tensor"),
            P("tensor", None),
            P(("dp", "tensor"), None),
        ),
        out_specs=(
            P(("dp", "tensor"), None),
            P(("dp", "tensor"), None),
            P("dp", None, "tensor"),
            P("tensor", "dp"),
        ),
        check_vma=False,
    )
```
